32 devices in a mesh: dp: 2 (over y), tm: 8 (over z, x), height: 2 (over core).
Axes of the slice: x: 2, y: 2, z: 4, core: 2. Of those that a mesh axis runs over, the one named last changes fastest.
Arguments:
- queries: bfloat16 [2, 16, 16, 8, 1536], P('dp', 'tm', 'height'), may hold values from -6 to 6
- keys: bfloat16 [2, 16, 16, 8, 1536], P('dp', 'tm', 'height'), may hold values from -6 to 6
- values: bfloat16 [2, 16, 16, 8, 1536], P('dp', 'tm', 'height'), may hold values from -6 to 6
- text_keys: bfloat16 [2, 256, 1536], P('dp'), may hold values from -110 to 110
- text_values: bfloat16 [2, 256, 1536], P('dp'), may hold values from -6 to 6
- gain_q: float32 [128], replicated, may hold values from 0.5 to 1.5
- gain_k: float32 [128], replicated, may hold values from 0.5 to 1.5
- window_ext: int32 [12, 3], replicated, may hold values from 0 to 1, as said below
- text_len: int32 [2], P('dp'), may hold values from 64 to 256, as said below
- out_grad: bfloat16 [2, 16, 16, 8, 1536], P('dp', 'tm', 'height'), may hold values from -60 to 60
Outputs:
- query_grad: bfloat16 [2, 16, 16, 8, 1536], P('dp', 'tm', 'height')
- key_grad: bfloat16 [2, 16, 16, 8, 1536], P('dp', 'tm', 'height')
- value_grad: bfloat16 [2, 16, 16, 8, 1536], P('dp', 'tm', 'height')
- text_key_grad: float32 [2, 256, 1536], P('dp')
- text_value_grad: float32 [2, 256, 1536], P('dp')
- gain_grads: float32 [2, 128], replicated
The draws below stay inside these ranges and needn't reach their ends.
Inputs may be any that keep to these rules, and one draw needn't show every extreme that they name: `window_ext`: along each of the three axes some head has reach 1. `text_len`: some sample has all 256 text tokens live.
All inputs are finite; a program needn't handle non-finite values.
Results may differ from the reference program's by a relative error of at most 0.0055.
The reference program's roundings to bfloat16 on the way count: a program that leaves them out, or rounds other values in their place, can miss the bound.
Values may be sent and summed in bfloat16 or wider, within the bound.
No kernel may reach another device: no remote copies, remote signals or barrier semaphores. Data moves between devices by JAX's collectives and lax.ppermute only.
A program may use at most 128 MiB of HBM per device.

```python
import jax
import jax.numpy as jnp
from jax import lax

HEADS = 12
HD = 128
TILE_F = 2
TILE_H = 4
TILE_W = 4
WT = 8
TXT = 256
HF = 1536
SAMPLES = 2
FRAMES = 16
ROWS = 16


def draw_queries(key, part):
    full_shape = (SAMPLES, FRAMES, ROWS, WT, HEADS, HD)
    subkey = jax.random.fold_in(key, 1)
    base_values = jnp.clip(jax.random.normal(subkey, full_shape, jnp.float32), -6.0, 6.0)
    return base_values.reshape(SAMPLES, FRAMES, ROWS, WT, HEADS * HD).astype(jnp.bfloat16)


def draw_text_keys(key, part):
    full_shape = (SAMPLES, TXT, HEADS, HD)
    subkey = jax.random.fold_in(key, 2)
    base_values = jnp.clip(jax.random.normal(subkey, full_shape, jnp.float32), -6.0, 6.0)
    return base_values.reshape(SAMPLES, TXT, HEADS * HD).astype(jnp.bfloat16)


def draw_out_grad(key, part):
    full_shape = (SAMPLES, FRAMES, ROWS, WT, HEADS * HD)
    subkey = jax.random.fold_in(key, 3)
    frame_scale = 1.0 + 2.0 * jnp.arange(FRAMES).astype(jnp.float32) / max(FRAMES - 1, 1)
    frame_scale = frame_scale[None, :, None, None, None]
    base_values = jnp.clip(jax.random.normal(subkey, full_shape, jnp.float32), -6.0, 6.0)
    return (base_values * frame_scale).astype(jnp.bfloat16)


def draw_window_ext(key, part):
    base_values = jax.random.randint(jax.random.fold_in(key, 5), (HEADS, 3), 0, 2)
    forced = jax.random.randint(jax.random.fold_in(key, 6), (3,), 0, HEADS)
    chosen = jnp.arange(HEADS)[:, None] == forced[None, :]
    return jnp.where(chosen, 1, base_values).astype(jnp.int32)


def draw_text_len(key, part):
    base_values = jax.random.randint(jax.random.fold_in(key, 7), (SAMPLES,), max(4, TXT // 4), TXT + 1)
    picked = jax.random.randint(jax.random.fold_in(key, 8), (), 0, SAMPLES)
    return jnp.where(jnp.arange(SAMPLES) == picked, TXT, base_values).astype(jnp.int32)


def block_scale(rng, shape, cuts, smallest, high):
    factor_of = 1.0
    for dim, shards_of in cuts:
        draws = jax.random.uniform(jax.random.fold_in(jax.random.fold_in(rng, 6), dim), (shards_of,), jnp.float32, smallest / len(cuts), high / len(cuts))
        factor_of = factor_of * jnp.repeat(jnp.exp(draws), shape[dim] // shards_of).reshape((-1,) + (1,) * (len(shape) - 1 - dim))
    return factor_of


def centred(own_key, dims, width, bound, shards=(), dtype=jnp.bfloat16):
    entries = width * jax.random.normal(own_key, dims, jnp.float32)
    if shards:
        entries = entries * block_scale(own_key, dims, shards, -0.22, 0.18)
    return jnp.clip(entries, -bound, bound).astype(dtype)


def setup_inputs(seed: int = 0) -> dict:
    key_list = jax.random.split(jax.random.key(seed), 11)
    return {
        "queries": draw_queries(jax.random.fold_in(key_list[10], 71), 0),
        "keys": centred(key_list[1], (SAMPLES, FRAMES, ROWS, WT, HF), 1.0, 6.0, ((0, 2), (1, 8), (2, 2))),
        "values": centred(key_list[2], (SAMPLES, FRAMES, ROWS, WT, HF), 1.0, 6.0, ((0, 2), (1, 8), (2, 2))),
        "text_keys": draw_text_keys(jax.random.fold_in(key_list[10], 71), 0),
        "text_values": centred(key_list[4], (SAMPLES, TXT, HF), 1.0, 6.0, ((0, 2),)),
        "gain_q": jnp.clip(1.0 + 0.1 * jax.random.normal(key_list[5], (HD,), jnp.float32), 0.5, 1.5),
        "gain_k": jnp.clip(1.0 + 0.1 * jax.random.normal(key_list[6], (HD,), jnp.float32), 0.5, 1.5),
        "window_ext": draw_window_ext(jax.random.fold_in(key_list[10], 71), 0),
        "text_len": draw_text_len(jax.random.fold_in(key_list[10], 71), 0),
        "out_grad": draw_out_grad(jax.random.fold_in(key_list[10], 71), 0),
    }


EPS = 1e-06

def normalize(raw_values, gain_vector, head_count):
    full_shape = raw_values.shape
    head_size = gain_vector.shape[0]
    split_values = raw_values.astype(jnp.float32).reshape(full_shape[:-1] + (head_count, head_size))
    inverse = lax.rsqrt(lax.optimization_barrier(jnp.mean(split_values * split_values, axis=-1, keepdims=True)) + EPS)
    scaled = (split_values * inverse * gain_vector).reshape(full_shape).astype(jnp.bfloat16)
    return (scaled, split_values, inverse)

def norm_backward(grad_out, split_values, inverse, gain_vector):
    full_shape = grad_out.shape
    grad_split = grad_out.reshape(split_values.shape)
    weighted = grad_split * gain_vector
    inner_mean = lax.optimization_barrier(jnp.mean(weighted * split_values, axis=-1, keepdims=True))
    grad_in = inverse * weighted - split_values * (inverse * inverse * inverse) * inner_mean
    gain_term = lax.optimization_barrier(jnp.sum((grad_split * split_values * inverse).reshape(-1, gain_vector.shape[0]), axis=0))
    return (grad_in.reshape(full_shape), gain_term)

def head_grads(query_head, key_head, value_head, grad_head, allowed):
    score_scale = query_head.shape[-1] ** (-0.5)
    scores = jnp.dot(query_head, key_head.T, preferred_element_type=jnp.float32) * score_scale
    scores = jnp.where(allowed, scores, -1e+30)
    peak_score = lax.optimization_barrier(jnp.max(scores, axis=-1, keepdims=True))
    weights = jnp.exp(scores - peak_score)
    weights = weights / lax.optimization_barrier(jnp.sum(weights, axis=-1, keepdims=True))
    weights_low = weights.astype(jnp.bfloat16)
    output = jnp.dot(weights_low, value_head, preferred_element_type=jnp.float32)
    delta_row = lax.optimization_barrier(jnp.sum(grad_head.astype(jnp.float32) * output, axis=-1, keepdims=True))
    value_part = jnp.dot(weights_low.T, grad_head, preferred_element_type=jnp.float32)
    prob_grad = jnp.dot(grad_head, value_head.T, preferred_element_type=jnp.float32)
    score_grad = (weights * (prob_grad - delta_row)).astype(jnp.bfloat16)
    query_part = jnp.dot(score_grad, key_head, preferred_element_type=jnp.float32) * score_scale
    key_part = jnp.dot(score_grad.T, query_head, preferred_element_type=jnp.float32) * score_scale
    return (query_part, key_part, value_part)

def tile_window(first_tiles, second_tiles, extent):
    within = jnp.abs(first_tiles[:, None, 0] - second_tiles[None, :, 0]) <= extent[0]
    within = within & (jnp.abs(first_tiles[:, None, 1] - second_tiles[None, :, 1]) <= extent[1])
    return within & (jnp.abs(first_tiles[:, None, 2] - second_tiles[None, :, 2]) <= extent[2])

def attend_all(query_flat, key_flat, value_flat, grad_flat, extents, query_tiles, key_tiles, key_valid, text_valid):
    head_count = extents.shape[0]
    head_size = query_flat.shape[1] // head_count
    text_count = text_valid.shape[0]

    def by_head(matrix):
        return matrix.reshape(matrix.shape[0], head_count, head_size).transpose(1, 0, 2)

    def per_head(operands):
        query_head, key_head, value_head, grad_head, extent = operands
        within = tile_window(query_tiles, key_tiles, extent)
        video_mask = within & key_valid[None, :]
        text_mask = jnp.broadcast_to(text_valid[None, :], (query_tiles.shape[0], text_count))
        allowed = jnp.concatenate([video_mask, text_mask], axis=1)
        return head_grads(query_head, key_head, value_head, grad_head, allowed)
    grad_query, grad_keys, grad_values = lax.map(per_head, (by_head(query_flat), by_head(key_flat), by_head(value_flat), by_head(grad_flat), extents))

    def merge_heads(stacked):
        return stacked.transpose(1, 0, 2).reshape(stacked.shape[1], -1)
    return (merge_heads(grad_query), merge_heads(grad_keys), merge_heads(grad_values))

def tile_coords(frame_index, row_index, column_index):
    full_shape = (frame_index.shape[0], row_index.shape[0], column_index.shape[0])
    pieces = [jnp.broadcast_to((frame_index // TILE_F)[:, None, None], full_shape), jnp.broadcast_to((row_index // TILE_H)[None, :, None], full_shape), jnp.broadcast_to((column_index // TILE_W)[None, None, :], full_shape)]
    return jnp.stack(pieces, axis=-1).reshape(-1, 3)

def reference(queries, keys, values, text_keys, text_values, gain_q, gain_k, window_ext, text_len, out_grad):
    head_count = window_ext.shape[0]
    frames_all, rows_all, columns_all, feature_count = queries.shape[1:]
    text_count = text_keys.shape[1]
    row_index = jnp.arange(rows_all).astype(jnp.int32)
    column_index = jnp.arange(columns_all).astype(jnp.int32)
    video_count = 3 * TILE_F * rows_all * columns_all

    def one_sample(sample_index):
        query_norm, query_split, query_inverse = normalize(queries[sample_index], gain_q, head_count)
        key_norm, key_split, key_inverse = normalize(keys[sample_index], gain_k, head_count)
        padding = ((TILE_F, TILE_F), (0, 0), (0, 0), (0, 0))
        key_padded = jnp.pad(key_norm, padding)
        value_padded = jnp.pad(values[sample_index], padding)
        grad_sample = out_grad[sample_index]
        text_valid = jnp.arange(text_count).astype(jnp.int32) < text_len[sample_index]

        def block_step(carried, block_index):
            key_acc, value_acc, text_key_acc, text_value_acc = carried
            frame_start = block_index * TILE_F
            query_block = lax.dynamic_slice_in_dim(query_norm, frame_start, TILE_F, 0).reshape(-1, feature_count)
            grad_block = lax.dynamic_slice_in_dim(grad_sample, frame_start, TILE_F, 0).reshape(-1, feature_count)
            key_block = lax.dynamic_slice_in_dim(key_padded, frame_start, 3 * TILE_F, 0).reshape(-1, feature_count)
            value_block = lax.dynamic_slice_in_dim(value_padded, frame_start, 3 * TILE_F, 0).reshape(-1, feature_count)
            query_frames = frame_start + jnp.arange(TILE_F).astype(jnp.int32)
            key_frames = frame_start - TILE_F + jnp.arange(3 * TILE_F).astype(jnp.int32)
            query_tiles = tile_coords(query_frames, row_index, column_index)
            key_tiles = tile_coords(key_frames, row_index, column_index)
            frame_valid = (key_frames >= 0) & (key_frames < frames_all)
            key_valid = jnp.broadcast_to(frame_valid[:, None, None], (3 * TILE_F, rows_all, columns_all)).reshape(-1)
            key_all = jnp.concatenate([key_block, text_keys[sample_index]], axis=0)
            value_all = jnp.concatenate([value_block, text_values[sample_index]], axis=0)
            grad_query, grad_keys, grad_values = attend_all(query_block, key_all, value_all, grad_block, window_ext, query_tiles, key_tiles, key_valid, text_valid)
            key_video = grad_keys[:video_count].reshape(3 * TILE_F, rows_all, columns_all, feature_count)
            value_video = grad_values[:video_count].reshape(3 * TILE_F, rows_all, columns_all, feature_count)
            key_acc = lax.dynamic_update_slice_in_dim(key_acc, lax.dynamic_slice_in_dim(key_acc, frame_start, 3 * TILE_F, 0) + key_video, frame_start, 0)
            value_acc = lax.dynamic_update_slice_in_dim(value_acc, lax.dynamic_slice_in_dim(value_acc, frame_start, 3 * TILE_F, 0) + value_video, frame_start, 0)
            text_key_acc = text_key_acc + grad_keys[video_count:]
            text_value_acc = text_value_acc + grad_values[video_count:]
            return ((key_acc, value_acc, text_key_acc, text_value_acc), grad_query)
        padded_zeros = jnp.zeros((frames_all + 2 * TILE_F, rows_all, columns_all, feature_count), jnp.float32)
        text_zeros = jnp.zeros((text_count, feature_count), jnp.float32)
        carried, query_blocks = lax.scan(block_step, (padded_zeros, padded_zeros, text_zeros, text_zeros), jnp.arange(frames_all // TILE_F).astype(jnp.int32))
        key_acc, value_acc, text_key_acc, text_value_acc = carried
        query_full = query_blocks.reshape(frames_all, rows_all, columns_all, feature_count)
        query_out, query_gain = norm_backward(query_full, query_split, query_inverse, gain_q)
        key_out, key_gain = norm_backward(key_acc[TILE_F:TILE_F + frames_all], key_split, key_inverse, gain_k)
        value_out = value_acc[TILE_F:TILE_F + frames_all]
        return (query_out.astype(jnp.bfloat16), key_out.astype(jnp.bfloat16), value_out.astype(jnp.bfloat16), text_key_acc, text_value_acc, jnp.stack([query_gain, key_gain]))
    results = lax.map(one_sample, jnp.arange(queries.shape[0]).astype(jnp.int32))
    return (results[0], results[1], results[2], results[3], results[4], lax.optimization_barrier(jnp.sum(results[5], axis=0)))
```

```python
import jax
import jax.numpy as jnp
from jax import lax
from jax.experimental import pallas as pl
from jax.experimental.pallas import tpu as pltpu
from jax.sharding import PartitionSpec as P

TILE_F = 2
TILE_H = 4
TILE_W = 4
EPS = 1e-06
HIDDEN = -1e30
LOG2E = 1.4426950408889634


VMEM = pl.BlockSpec(memory_space=pltpu.VMEM)
F32 = jnp.float32
BF16 = jnp.bfloat16


def dot(x, y, dims):
    return lax.dot_general(x, y, ((dims[:1], dims[1:]), ((), ())), preferred_element_type=F32)


def pack_pairs(place, first, second, members):
    tokens, features = first.shape
    width = features // 4

    def kernel(place_ref, first_ref, second_ref, *out_refs):
        for out_ref, j in zip(out_refs, members):
            start = pl.multiple_of((place_ref[0] ^ j) * width, 128)
            out_ref[0] = first_ref[:, pl.ds(start, width)]
            out_ref[1] = second_ref[:, pl.ds(start, width)]

    shape = jax.ShapeDtypeStruct((2, tokens, width), first.dtype)
    return pl.pallas_call(
        kernel,
        grid_spec=pltpu.PrefetchScalarGridSpec(
            num_scalar_prefetch=1, grid=(), in_specs=[VMEM] * 2, out_specs=[VMEM] * len(members)
        ),
        out_shape=[shape] * len(members),
        name="pack",
    )(place, first, second)


def unpack(place, pieces, dtype):
    count, rows, width = pieces[0].shape

    def kernel(place_ref, *refs):
        for j in range(4):
            start = pl.multiple_of((place_ref[0] ^ j) * width, 128)
            for i in range(count):
                refs[4 + i][:, pl.ds(start, width)] = refs[j][i].astype(dtype)

    return pl.pallas_call(
        kernel,
        grid_spec=pltpu.PrefetchScalarGridSpec(
            num_scalar_prefetch=1, grid=(), in_specs=[VMEM] * 4, out_specs=[VMEM] * count
        ),
        out_shape=[jax.ShapeDtypeStruct((rows, 4 * width), dtype)] * count,
        name="unpack",
    )(place, *pieces)


def attention_kernel(half, columns, slot, text_count, scale):
    tile = 2 * slot
    video = 4 * tile
    tile_rows = half // TILE_H
    tile_cols = columns // TILE_W
    codes = 2 * tile_rows * tile_cols

    def unit(x):
        x = x.astype(F32)
        inverse = lax.rsqrt(jnp.mean(x * x, axis=-1, keepdims=True) + EPS)
        return x * inverse, inverse

    def place_of(shape):
        n = lax.broadcasted_iota(jnp.int32, shape, 0)
        row = (n // columns) % half
        return (n // slot) * tile_rows + row // TILE_H, (n % columns) // TILE_W

    def kernel(
        place_ref, ext_ref, len_ref,
        q0, k0, v0, d0, kv1, kv2, kv3, qd1, qd2, qd3, ha0, ha1, hb0, hb1, tk, tv, gq_ref, gk_ref,
        oq0, oq1, oq2, oq3, own, oha, ohb, otext, ogain,
        kn, vs, kx, qn, ds_, qx, qr, dk, dv, oq,
    ):
        h = pl.program_id(0)
        g, p, last = place_ref[0], place_ref[1], place_ref[2]
        a, b = g >> 1, g & 1
        head = 3 * g + h
        e0, e1, e2 = ext_ref[head, 0], ext_ref[head, 1], ext_ref[head, 2]
        gq, gk = gq_ref[...], gk_ref[...]
        spot = lambda start: pl.ds(pl.multiple_of(start, slot), slot)
        own_at = [(g ^ j) * slot for j in range(4)]
        a_base = jnp.where(a == 0, 3 * tile, 0)
        b_base = jnp.where(a == 0, 0, 3 * tile)
        halo_at = [a_base + b * slot, a_base + (1 - b) * slot, b_base + b * slot, b_base + (1 - b) * slot]

        key_parts = [(k0[...], v0[...])] + [(r[0], r[1]) for r in (kv1, kv2, kv3)]
        key_parts = [(x, y, at + tile) for (x, y), at in zip(key_parts, own_at)]
        key_parts += [(r[0], r[1], at) for r, at in zip((ha0, ha1, hb0, hb1), halo_at)]
        for x, y, at in key_parts:
            hat, _ = unit(x)
            kx[spot(at), :] = hat
            kn[spot(at), :128] = (hat * gk).astype(BF16)
            vs[spot(at), :] = y
        kn[video:, :128] = tk[...]
        vs[video:, :] = tv[...]
        for (x, y), at in zip([(q0[...], d0[...])] + [(r[0], r[1]) for r in (qd1, qd2, qd3)], own_at):
            hat, inverse = unit(x)
            qx[spot(at), :] = hat
            qr[spot(at), :] = jnp.broadcast_to(inverse, hat.shape)
            qn[spot(at), :128] = (hat * gq).astype(BF16)
            ds_[spot(at), :] = y

        lane = lax.broadcasted_iota(jnp.int32, (tile, 128), 1)
        row, col = place_of((tile, 128))
        code = row * tile_cols + col
        space = 2 * tile_rows * tile_cols
        code_t, code_s = lane // space, lane % space
        code_r, code_c = code_s // tile_cols, code_s % tile_cols
        near = (jnp.abs(row - code_r) <= e1) & (jnp.abs(col - code_c) <= e2)

        @pl.when(h == 0)
        def _():
            for t in range(2):
                qn[t * tile:(t + 1) * tile, 128:] = jnp.where(lane == t * space + code, 1.0, 0.0).astype(BF16)

        for block in range(4):
            seen = near & (jnp.abs(block - 1 - code_t) <= e0)
            if block == 0:
                seen = seen & (p > 0)
            if block == 3:
                seen = seen & (p < last)
            kn[block * tile:(block + 1) * tile, 128:] = jnp.where(seen, 0.0, HIDDEN).astype(BF16)
        word = lax.broadcasted_iota(jnp.int32, (text_count, 128), 0)
        kn[video:, 128:] = jnp.where(word < len_ref[0], 0.0, HIDDEN).astype(BF16)

        gain_q = jnp.zeros((1, 128), F32)
        for t in range(2):
            window, words = slice(t * tile, (t + 3) * tile), slice(video, video + text_count)
            query, grad = qn[t * tile:(t + 1) * tile, :], ds_[t * tile:(t + 1) * tile, :]
            parts = (window, words)
            scores = [dot(kn[x, :], query, (1, 1)) for x in parts]
            top = jnp.maximum(*[jnp.max(s, axis=0, keepdims=True) for s in scores])
            powers = [jnp.exp2((s - top) * (scale * LOG2E)) for s in scores]
            total = sum(jnp.sum(e, axis=0, keepdims=True) for e in powers)
            share = 1.0 / total
            probs = [e * share for e in powers]
            low = [x.astype(BF16) for x in probs]
            attn = sum(dot(vs[x, :], w, (0, 0)) for x, w in zip(parts, low))
            delta = jnp.sum(grad.astype(F32).T * attn, axis=0, keepdims=True)
            prob_grad = [dot(vs[x, :], grad, (1, 1)) for x in parts]
            score_grad = [(w * (y - delta)).astype(BF16) for w, y in zip(probs, prob_grad)]
            dqn = sum(dot(kn[x, :128], s, (0, 0)) for x, s in zip(parts, score_grad)).T * scale
            for x, w, s in zip(parts, low, score_grad):
                value_part = dot(w, grad, (1, 0))
                key_part = dot(s, query[:, :128], (1, 0)) * scale
                if t == 0:
                    dv[x, :] = value_part
                    dk[x, :] = key_part
                elif x is words:
                    dv[x, :] += value_part
                    dk[x, :] += key_part
                else:
                    dv[tile:3 * tile, :] += value_part[:2 * tile]
                    dk[tile:3 * tile, :] += key_part[:2 * tile]
                    dv[3 * tile:video, :] = value_part[2 * tile:]
                    dk[3 * tile:video, :] = key_part[2 * tile:]
            rows = slice(t * tile, (t + 1) * tile)
            hat = qx[rows, :]
            weighted = dqn * gq
            inner = jnp.mean(weighted * hat, axis=-1, keepdims=True)
            oq[rows, :] = (qr[rows, :] * (weighted - hat * inner)).astype(BF16)
            gain_q = gain_q + jnp.sum(dqn * hat, axis=0, keepdims=True)
        gain_k = jnp.sum(dk[:video, :] * kx[...], axis=0, keepdims=True)
        gains = jnp.concatenate([gain_q, gain_k], axis=0)

        @pl.when(h == 0)
        def _():
            ogain[...] = gains

        @pl.when(h > 0)
        def _():
            ogain[...] += gains

        for j, out in enumerate((oq0, oq1, oq2, oq3)):
            out[0] = oq[spot(own_at[j]), :]
            own[0, j] = dk[spot(own_at[j] + tile), :]
            own[1, j] = dv[spot(own_at[j] + tile), :]
        for i in range(2):
            oha[0, i] = dk[spot(halo_at[i]), :]
            oha[1, i] = dv[spot(halo_at[i]), :]
            ohb[0, i] = dk[spot(halo_at[2 + i]), :]
            ohb[1, i] = dv[spot(halo_at[2 + i]), :]
        otext[0] = dk[video:, :]
        otext[1] = dv[video:, :]

    return kernel


def attention(place, window_ext, text_len, own, keys_in, queries_in, halos, text_keys, text_values, gain_q, gain_k, dims):
    half, columns = dims
    slot, features = own[0].shape
    width = features // 4
    heads = width // 128
    text_count = text_keys.shape[0]
    tile = 2 * slot
    mine = pl.BlockSpec((slot, 128), lambda h, pr, er, lr: (0, pr[0] * heads + h))
    pair = pl.BlockSpec((2, slot, 128), lambda h, pr, er, lr: (0, 0, h))
    text = pl.BlockSpec((text_count, 128), lambda h, pr, er, lr: (0, pr[0] * heads + h))
    gain = pl.BlockSpec((1, 128), lambda h, pr, er, lr: (0, 0))
    out_q = pl.BlockSpec((1, slot, 128), lambda h, pr, er, lr: (0, 0, h))
    s = jax.ShapeDtypeStruct
    return pl.pallas_call(
        attention_kernel(half, columns, slot, text_count, 128 ** -0.5),
        grid_spec=pltpu.PrefetchScalarGridSpec(
            num_scalar_prefetch=3,
            grid=(heads,),
            in_specs=[mine] * 4 + [pair] * 10 + [text] * 2 + [gain] * 2,
            out_specs=[out_q] * 4
            + [
                pl.BlockSpec((2, 4, slot, 128), lambda h, pr, er, lr: (0, 0, 0, h)),
                pl.BlockSpec((2, 2, slot, 128), lambda h, pr, er, lr: (0, 0, 0, h)),
                pl.BlockSpec((2, 2, slot, 128), lambda h, pr, er, lr: (0, 0, 0, h)),
                pl.BlockSpec((2, text_count, 128), lambda h, pr, er, lr: (0, 0, h)),
                pl.BlockSpec((2, 128), lambda h, pr, er, lr: (0, 0)),
            ],
            scratch_shapes=[
                pltpu.VMEM((4 * tile + text_count, 256), BF16),
                pltpu.VMEM((4 * tile + text_count, 128), BF16),
                pltpu.VMEM((4 * tile, 128), F32),
                pltpu.VMEM((2 * tile, 256), BF16),
                pltpu.VMEM((2 * tile, 128), BF16),
                pltpu.VMEM((2 * tile, 128), F32),
                pltpu.VMEM((2 * tile, 128), F32),
                pltpu.VMEM((4 * tile + text_count, 128), F32),
                pltpu.VMEM((4 * tile + text_count, 128), F32),
                pltpu.VMEM((2 * tile, 128), BF16),
            ],
        ),
        out_shape=[s((1, slot, width), BF16)] * 4
        + [
            s((2, 4, slot, width), F32),
            s((2, 2, slot, width), F32),
            s((2, 2, slot, width), F32),
            s((2, text_count, width), F32),
            s((2, 128), F32),
        ],
        name="attention",
    )(place, window_ext, text_len, *own, *keys_in, *queries_in, *halos, text_keys, text_values, gain_q, gain_k)


def finish(place, own, back_a, back_b, key_flat, keys_in, gain_k):
    slot = key_flat.shape[0]
    width = own.shape[-1]
    heads = width // 128

    def kernel(place_ref, own_ref, a_ref, b_ref, k0, kv1, kv2, kv3, gk_ref, *outs):
        gk = gk_ref[...]
        for j, out in enumerate(outs):
            back = (a_ref, b_ref)[j // 2]
            x = (k0[...] if j == 0 else (kv1, kv2, kv3)[j - 1][0]).astype(F32)
            inverse = lax.rsqrt(jnp.mean(x * x, axis=-1, keepdims=True) + EPS)
            hat = x * inverse
            weighted = (own_ref[0, j] + back[0, j % 2]) * gk
            inner = jnp.mean(weighted * hat, axis=-1, keepdims=True)
            out[0] = (inverse * (weighted - hat * inner)).astype(BF16)
            out[1] = (own_ref[1, j] + back[1, j % 2]).astype(BF16)

    pair = pl.BlockSpec((2, slot, 128), lambda h, pr: (0, 0, h))
    back = pl.BlockSpec((2, 2, slot, 128), lambda h, pr: (0, 0, 0, h))
    return pl.pallas_call(
        kernel,
        grid_spec=pltpu.PrefetchScalarGridSpec(
            num_scalar_prefetch=1,
            grid=(heads,),
            in_specs=[
                pl.BlockSpec((2, 4, slot, 128), lambda h, pr: (0, 0, 0, h)),
                back,
                back,
                pl.BlockSpec((slot, 128), lambda h, pr: (0, pr[0] * heads + h)),
                pair,
                pair,
                pair,
                pl.BlockSpec((1, 128), lambda h, pr: (0, 0)),
            ],
            out_specs=[pair] * 4,
        ),
        out_shape=[jax.ShapeDtypeStruct((2, slot, width), BF16)] * 4,
        name="finish",
    )(place, own, back_a, back_b, key_flat, *keys_in, gain_k)


def local(queries, keys, values, text_keys, text_values, gain_q, gain_k, window_ext, text_len, out_grad):
    head_count = window_ext.shape[0]
    frames, half, columns, features = queries.shape[1:]
    text_count = text_keys.shape[1]
    peers, heights = lax.axis_size("tm"), lax.axis_size("height")
    quads = peers // 2
    assert frames == TILE_F and heights == 2 and peers % 2 == 0
    assert features == 128 * head_count and head_count % 4 == 0
    assert half % TILE_H == 0 and columns % TILE_W == 0 and text_count % (8 * quads) == 0
    axes = ("tm", "height")
    me = lax.axis_index("tm")
    quad = me // 2
    member = (me % 2) * 2 + lax.axis_index("height")
    place = jnp.stack([member, quad, jnp.full_like(quad, quads - 1)]).astype(jnp.int32)

    def swap(x, j):
        return lax.ppermute(x, axes, [(4 * n + m, 4 * n + (m ^ j)) for n in range(quads) for m in range(4)])

    def move(x, step):
        pairs = [(4 * n + m, 4 * (n + step(m // 2)) + m) for n in range(quads) for m in range(4)]
        return lax.ppermute(x, axes, [(i, j) for i, j in pairs if 0 <= j < 4 * quads])

    out_a, out_b = (lambda a: 2 * a - 1), (lambda a: 1 - 2 * a)
    flat = [x.reshape(-1, features) for x in (queries, keys, values, out_grad)]
    q, k, v, d = flat
    gq, gk = gain_q.reshape(1, -1), gain_k.reshape(1, -1)

    kv = pack_pairs(place, k, v, (0, 1, 2, 3))
    kv_in = [swap(kv[j], j) for j in (2, 3, 1)]
    kv_in = [kv_in[2], kv_in[0], kv_in[1]]
    halos = [move(kv[0], out_a)]
    qd = pack_pairs(place, q, d, (1, 2, 3))
    qd_in = [swap(x, j) for x, j in zip(qd, (1, 2, 3))]
    halos += [move(kv_in[0], out_a), move(kv_in[1], out_b), move(kv_in[2], out_b)]

    oq0, oq1, oq2, oq3, own, halo_a, halo_b, text, gains = attention(
        place, window_ext, text_len, flat, kv_in, qd_in, halos, text_keys[0], text_values[0], gq, gk, (half, columns)
    )

    back_a = move(halo_a, out_b)
    back_b = move(halo_b, out_a)
    oq_in = [swap(x, j) for x, j in zip((oq1, oq2, oq3), (1, 2, 3))]
    gain_total = lax.psum(gains, ("dp", "tm", "height"))

    whole = jnp.zeros((2, text_count, features), F32)
    whole = lax.dynamic_update_slice(whole, text, (0, 0, member * (features // 4)))
    text_sum = lax.psum(whole, axes)

    query_out = unpack(place, [oq0] + oq_in, BF16)[0]
    ended = finish(place, own, back_a, back_b, k, kv_in, gk)
    ended_in = [swap(x, j) for x, j in zip(ended[1:], (1, 2, 3))]
    key_out, value_out = unpack(place, [ended[0]] + ended_in, BF16)
    shape = queries.shape
    return (
        query_out.reshape(shape),
        key_out.reshape(shape),
        value_out.reshape(shape),
        text_sum[0][None],
        text_sum[1][None],
        gain_total,
    )


def solution(mesh):
    tokens = P("dp", "tm", "height", None, None)
    words = P("dp", None, None)
    return jax.shard_map(
        local,
        mesh=mesh,
        in_specs=(tokens, tokens, tokens, words, words, P(), P(), P(), P("dp"), tokens),
        out_specs=(tokens, tokens, tokens, words, words, P()),
        check_vma=False,
    )
```

```python
import jax
import jax.numpy as jnp
from jax import lax
from jax.experimental import pallas as pl
from jax.experimental.pallas import tpu as pltpu
from jax.sharding import PartitionSpec as P

TILE_F = 2
TILE_H = 4
TILE_W = 4
EPS = 1e-06
HIDDEN = -1e30
LOG2E = 1.4426950408889634


VMEM = pl.BlockSpec(memory_space=pltpu.VMEM)
F32 = jnp.float32
BF16 = jnp.bfloat16


def dot(x, y, dims):
    return lax.dot_general(x, y, ((dims[:1], dims[1:]), ((), ())), preferred_element_type=F32)


def pack(place, arrays, groups):
    tokens, features = arrays[0].shape
    width = features // 4

    def kernel(place_ref, *refs):
        for out_ref, (j, picked) in zip(refs[len(arrays):], groups):
            start = pl.multiple_of((place_ref[0] ^ j) * width, 128)
            for i, n in enumerate(picked):
                out_ref[i] = refs[n][:, pl.ds(start, width)]

    return pl.pallas_call(
        kernel,
        grid_spec=pltpu.PrefetchScalarGridSpec(
            num_scalar_prefetch=1, grid=(), in_specs=[VMEM] * len(arrays), out_specs=[VMEM] * len(groups)
        ),
        out_shape=[jax.ShapeDtypeStruct((len(picked), tokens, width), arrays[0].dtype) for _, picked in groups],
        name="pack",
    )(place, *arrays)


def unpack(place, pieces, dtype):
    count, rows, width = pieces[0].shape

    def kernel(place_ref, *refs):
        for j in range(4):
            start = pl.multiple_of((place_ref[0] ^ j) * width, 128)
            for i in range(count):
                refs[4 + i][:, pl.ds(start, width)] = refs[j][i].astype(dtype)

    return pl.pallas_call(
        kernel,
        grid_spec=pltpu.PrefetchScalarGridSpec(
            num_scalar_prefetch=1, grid=(), in_specs=[VMEM] * 4, out_specs=[VMEM] * count
        ),
        out_shape=[jax.ShapeDtypeStruct((rows, 4 * width), dtype)] * count,
        name="unpack",
    )(place, *pieces)


def unit(x):
    x = x.astype(F32)
    inverse = lax.rsqrt(jnp.mean(x * x, axis=-1, keepdims=True) + EPS)
    return x * inverse, inverse


def spatial(half, columns, slot, ext1, ext2):
    shape = (2 * slot, 128)
    tile_rows, tile_cols = half // TILE_H, columns // TILE_W
    n = lax.broadcasted_iota(jnp.int32, shape, 0)
    row = (n // slot) * tile_rows + ((n // columns) % half) // TILE_H
    col = (n % columns) // TILE_W
    lane = lax.broadcasted_iota(jnp.int32, shape, 1)
    space = 2 * tile_rows * tile_cols
    code = lane % space
    near = (jnp.abs(row - code // tile_cols) <= ext1) & (jnp.abs(col - code % tile_cols) <= ext2)
    return near, lane, row * tile_cols + col, space


def hidden(seen):
    return jnp.where(seen, 0.0, HIDDEN).astype(BF16)


def attention_kernel(half, columns, slot, text_count, chunks, scale):
    tile = 2 * slot
    video = 4 * tile
    chunk = text_count // chunks

    def kernel(place_ref, ext_ref, len_ref, *refs):
        q0, k0, v0, d0, near1, kv2, kv3, qd1, qd2, qd3, ha0, ha1, hb0, hb1, tk, tv, gq_ref, gk_ref = refs[:18]
        oq0, oq1, oq2, oq3, own, stats0, stats1, ogain = refs[18:26]
        texts = refs[26:26 + chunks]
        kn, vs, qn, grads, qx, qr, dk, dv, oq = refs[26 + chunks:]
        h = pl.program_id(0)
        g, p, last = place_ref[0], place_ref[1], place_ref[2]
        a, b = g >> 1, g & 1
        head = 3 * g + h
        e0, e1, e2 = ext_ref[head, 0], ext_ref[head, 1], ext_ref[head, 2]
        gq, gk = gq_ref[...], gk_ref[...]
        spot = lambda start: pl.ds(pl.multiple_of(start, slot), slot)
        own_at = [(g ^ j) * slot for j in range(4)]
        a_base = jnp.where(a == 0, 3 * tile, 0)
        b_base = jnp.where(a == 0, 0, 3 * tile)
        halo_at = [a_base + b * slot, a_base + (1 - b) * slot, b_base + b * slot, b_base + (1 - b) * slot]

        key_parts = [(k0[...], v0[...])] + [(r[0], r[1]) for r in (near1, kv2, kv3)]
        key_parts = [(x, y, at + tile) for (x, y), at in zip(key_parts, own_at)]
        key_parts += [(r[0], r[1], at) for r, at in zip((ha0, ha1, hb0, hb1), halo_at)]
        for x, y, at in key_parts:
            kn[spot(at), :128] = (unit(x)[0] * gk).astype(BF16)
            vs[spot(at), :] = y
        kn[video:, :128] = tk[...]
        vs[video:, :] = tv[...]
        for (x, y), at in zip([(q0[...], d0[...])] + [(r[0], r[1]) for r in (qd1, qd2, qd3)], own_at):
            hat, inverse = unit(x)
            qx[spot(at), :] = hat
            qr[spot(at), :] = jnp.broadcast_to(inverse, hat.shape)
            qn[spot(at), :128] = (hat * gq).astype(BF16)
            grads[spot(at), :] = y

        near, lane, code, space = spatial(half, columns, slot, e1, e2)

        @pl.when(h == 0)
        def _():
            for t in range(2):
                qn[t * tile:(t + 1) * tile, 128:] = jnp.where(lane == t * space + code, 1.0, 0.0).astype(BF16)

        for block in range(4):
            seen = near & (jnp.abs(block - 1 - lane // space) <= e0)
            if block == 0:
                seen = seen & (p > 0)
            if block == 3:
                seen = seen & (p < last)
            kn[block * tile:(block + 1) * tile, 128:] = hidden(seen)
        word = lax.broadcasted_iota(jnp.int32, (text_count, 128), 0)
        kn[video:, 128:] = hidden(word < len_ref[0])

        gain_q = jnp.zeros((1, 128), F32)
        for t, stats in enumerate((stats0, stats1)):
            parts = (slice(t * tile, (t + 3) * tile), slice(video, video + text_count))
            rows = slice(t * tile, (t + 1) * tile)
            query, grad = qn[rows, :], grads[rows, :]
            scores = [dot(kn[x, :], query, (1, 1)) for x in parts]
            top = jnp.maximum(*[jnp.max(s, axis=0, keepdims=True) for s in scores])
            powers = [jnp.exp2((s - top) * (scale * LOG2E)) for s in scores]
            share = 1.0 / sum(jnp.sum(e, axis=0, keepdims=True) for e in powers)
            probs = [e * share for e in powers]
            low = [x.astype(BF16) for x in probs]
            attn = sum(dot(vs[x, :], w, (0, 0)) for x, w in zip(parts, low))
            delta = jnp.sum(grad.astype(F32).T * attn, axis=0, keepdims=True)
            stats[...] = jnp.zeros_like(stats)
            stats[0, 0:1, :] = top
            stats[0, 1:2, :] = share
            stats[0, 2:3, :] = delta
            prob_grad = [dot(vs[x, :], grad, (1, 1)) for x in parts]
            score_grad = [(w * (y - delta)).astype(BF16) for w, y in zip(probs, prob_grad)]
            dqn = sum(dot(kn[x, :128], s, (0, 0)) for x, s in zip(parts, score_grad)).T * scale
            mine = slice((1 - t) * tile, (3 - t) * tile)
            for x, w, s in ((slice(0, 2 * tile), low[0][mine], score_grad[0][mine]), (slice(2 * tile, None), low[1], score_grad[1])):
                value_part = dot(w, grad, (1, 0))
                key_part = dot(s, query[:, :128], (1, 0)) * scale
                if t == 0:
                    dv[x, :] = value_part
                    dk[x, :] = key_part
                else:
                    dv[x, :] += value_part
                    dk[x, :] += key_part
            hat = qx[rows, :]
            weighted = dqn * gq
            inner = jnp.mean(weighted * hat, axis=-1, keepdims=True)
            oq[rows, :] = (qr[rows, :] * (weighted - hat * inner)).astype(BF16)
            gain_q = gain_q + jnp.sum(dqn * hat, axis=0, keepdims=True)

        @pl.when(h == 0)
        def _():
            ogain[...] = gain_q

        @pl.when(h > 0)
        def _():
            ogain[...] += gain_q

        for j, out in enumerate((oq0, oq1, oq2, oq3)):
            out[0] = oq[spot(own_at[j]), :]
        own[0] = dk[:2 * tile, :]
        own[1] = dv[:2 * tile, :]
        for d, out in enumerate(texts):
            start = pl.multiple_of(2 * tile + lax.rem(p + d, chunks) * chunk, 8)
            out[0] = dk[pl.ds(start, chunk), :]
            out[1] = dv[pl.ds(start, chunk), :]

    return kernel


def attention(place, window_ext, text_len, own, near1, kv_in, qd_in, halos, text_keys, text_values, gain_q, gain_k, dims):
    half, columns, chunks = dims
    slot, features = own[0].shape
    width = features // 4
    heads = width // 128
    text_count = text_keys.shape[0]
    tile = 2 * slot
    mine = pl.BlockSpec((slot, 128), lambda h, pr, er, lr: (0, pr[0] * heads + h))
    front = pl.BlockSpec((2, slot, 128), lambda h, pr, er, lr: (0, 0, h))
    back = pl.BlockSpec((2, slot, 128), lambda h, pr, er, lr: (1, 0, h))
    text = pl.BlockSpec((text_count, 128), lambda h, pr, er, lr: (0, pr[0] * heads + h))
    fixed = pl.BlockSpec((1, 128), lambda h, pr, er, lr: (0, 0))
    stats = pl.BlockSpec((1, 8, tile), lambda h, pr, er, lr: (h, 0, 0))
    s = jax.ShapeDtypeStruct
    return pl.pallas_call(
        attention_kernel(half, columns, slot, text_count, chunks, 128 ** -0.5),
        grid_spec=pltpu.PrefetchScalarGridSpec(
            num_scalar_prefetch=3,
            grid=(heads,),
            in_specs=[mine] * 4 + [front] * 3 + [back] + [front] * 6 + [text] * 2 + [fixed] * 2,
            out_specs=[front_of(slot)] * 4
            + [pl.BlockSpec((2, 2 * tile, 128), lambda h, pr, er, lr: (0, 0, h)), stats, stats, fixed]
            + [pl.BlockSpec((2, text_count // chunks, 128), lambda h, pr, er, lr: (0, 0, h))] * chunks,
            scratch_shapes=[
                pltpu.VMEM((4 * tile + text_count, 256), BF16),
                pltpu.VMEM((4 * tile + text_count, 128), BF16),
                pltpu.VMEM((2 * tile, 256), BF16),
                pltpu.VMEM((2 * tile, 128), BF16),
                pltpu.VMEM((2 * tile, 128), F32),
                pltpu.VMEM((2 * tile, 128), F32),
                pltpu.VMEM((2 * tile + text_count, 128), F32),
                pltpu.VMEM((2 * tile + text_count, 128), F32),
                pltpu.VMEM((2 * tile, 128), BF16),
            ],
        ),
        out_shape=[s((1, slot, width), BF16)] * 4
        + [s((2, 2 * tile, width), F32), s((heads, 8, tile), F32), s((heads, 8, tile), F32), s((1, 128), F32)]
        + [s((2, text_count // chunks, width), F32)] * chunks,
        name="attention",
    )(place, window_ext, text_len, *own, near1, *kv_in, near1, *qd_in, *halos, text_keys, text_values, gain_q, gain_k)


def front_of(slot):
    return pl.BlockSpec((1, slot, 128), lambda h, pr, er, lr: (0, 0, h))


def edges(place, window_ext, own, stats, k, v, near1, kv_in, halos, gain_q, gain_k, gain_in, dims):
    half, columns = dims
    slot, features = k.shape
    width = features // 4
    heads = width // 128
    tile = 2 * slot
    scale = 128 ** -0.5

    def kernel(
        place_ref, ext_ref, own_ref, before_ref, after_ref, k0, v0, kv1, kv2, kv3, ha0, ha1, hb0, hb1,
        gq_ref, gk_ref, gain_ref, o0, o1, o2, o3, ogain, kn, vs, kx, kr, qn, grads, ends,
    ):
        h = pl.program_id(0)
        g, p, last = place_ref[0], place_ref[1], place_ref[2]
        a, b = g >> 1, g & 1
        head = 3 * g + h
        e0, e1, e2 = ext_ref[head, 0], ext_ref[head, 1], ext_ref[head, 2]
        gq, gk = gq_ref[...], gk_ref[...]
        spot = lambda start: pl.ds(pl.multiple_of(start, slot), slot)
        own_at = [(g ^ j) * slot for j in range(4)]
        a_base, b_base = (1 - a) * tile, a * tile
        halo_at = [a_base + b * slot, a_base + (1 - b) * slot, b_base + b * slot, b_base + (1 - b) * slot]
        for (x, y), at in zip([(k0[...], v0[...])] + [(r[0], r[1]) for r in (kv1, kv2, kv3)], own_at):
            hat, inverse = unit(x)
            kx[spot(at), :] = hat
            kr[spot(at), :] = jnp.broadcast_to(inverse, hat.shape)
            kn[spot(at), :128] = (hat * gk).astype(BF16)
            vs[spot(at), :] = y
        for r, at in zip((ha0, ha1, hb0, hb1), halo_at):
            qn[spot(at), :128] = (unit(r[0])[0] * gq).astype(BF16)
            grads[spot(at), :] = r[1]
        near, lane, code, space = spatial(half, columns, slot, e1, e2)
        near = near & (e0 >= 1)
        for t in range(2):
            kn[t * tile:(t + 1) * tile, 128:] = hidden(near & ((p > 0) if t == 0 else (p < last)))

        @pl.when(h == 0)
        def _():
            for t in range(2):
                qn[t * tile:(t + 1) * tile, 128:] = jnp.where(lane == code, 1.0, 0.0).astype(BF16)

        gain_k = jnp.zeros((1, 128), F32)
        for t, stats_ref in enumerate((before_ref, after_ref)):
            rows = slice(t * tile, (t + 1) * tile)
            top, share, delta = stats_ref[0, 0:1, :], stats_ref[0, 1:2, :], stats_ref[0, 2:3, :]
            query, grad = qn[rows, :], grads[rows, :]
            probs = jnp.exp2((dot(kn[rows, :], query, (1, 1)) - top) * (scale * LOG2E)) * share
            prob_grad = dot(vs[rows, :], grad, (1, 1))
            score_grad = (probs * (prob_grad - delta)).astype(BF16)
            value_sum = own_ref[1, rows, :] + dot(probs.astype(BF16), grad, (1, 0))
            key_sum = own_ref[0, rows, :] + dot(score_grad, query[:, :128], (1, 0)) * scale
            hat = kx[rows, :]
            weighted = key_sum * gk
            inner = jnp.mean(weighted * hat, axis=-1, keepdims=True)
            ends[0, rows, :] = (kr[rows, :] * (weighted - hat * inner)).astype(BF16)
            ends[1, rows, :] = value_sum.astype(BF16)
            gain_k = gain_k + jnp.sum(key_sum * hat, axis=0, keepdims=True)

        @pl.when(h == 0)
        def _():
            ogain[0:1, :] = gain_ref[...]
            ogain[1:2, :] = gain_k

        @pl.when(h > 0)
        def _():
            ogain[1:2, :] += gain_k

        for j, out in enumerate((o0, o1, o2, o3)):
            out[0] = ends[0, spot(own_at[j]), :]
            out[1] = ends[1, spot(own_at[j]), :]

    mine = pl.BlockSpec((slot, 128), lambda h, pr, er: (0, pr[0] * heads + h))
    front = pl.BlockSpec((2, slot, 128), lambda h, pr, er: (0, 0, h))
    back = pl.BlockSpec((2, slot, 128), lambda h, pr, er: (1, 0, h))
    fixed = pl.BlockSpec((1, 128), lambda h, pr, er: (0, 0))
    stat = pl.BlockSpec((1, 8, tile), lambda h, pr, er: (h, 0, 0))
    s = jax.ShapeDtypeStruct
    return pl.pallas_call(
        kernel,
        grid_spec=pltpu.PrefetchScalarGridSpec(
            num_scalar_prefetch=2,
            grid=(heads,),
            in_specs=[pl.BlockSpec((2, 2 * tile, 128), lambda h, pr, er: (0, 0, h)), stat, stat, mine, mine]
            + [front] * 3
            + [back] * 2
            + [front] * 2
            + [fixed] * 3,
            out_specs=[front] * 4 + [pl.BlockSpec((2, 128), lambda h, pr, er: (0, 0))],
            scratch_shapes=[
                pltpu.VMEM((2 * tile, 256), BF16),
                pltpu.VMEM((2 * tile, 128), BF16),
                pltpu.VMEM((2 * tile, 128), F32),
                pltpu.VMEM((2 * tile, 128), F32),
                pltpu.VMEM((2 * tile, 256), BF16),
                pltpu.VMEM((2 * tile, 128), BF16),
                pltpu.VMEM((2, 2 * tile, 128), BF16),
            ],
        ),
        out_shape=[s((2, slot, width), BF16)] * 4 + [s((2, 128), F32)],
        name="edges",
    )(place, window_ext, own, *stats, k, v, near1, *kv_in, *halos, gain_q, gain_k, gain_in)


def text_chunk(parts, gains):
    _, rows, width = parts[0].shape

    def kernel(*refs):
        out_ref = refs[-1]
        total = refs[0][...]
        for ref in refs[1:-2]:
            total = total + ref[...]
        out_ref[:, :rows, :] = total.astype(BF16)
        out_ref[:, rows:, :] = jnp.zeros((2, 8, width), BF16)
        rest = refs[-2][...]
        for i in range(3):
            part = rest.astype(BF16)
            out_ref[0, rows + 2 * i:rows + 2 * i + 2, :128] = part
            rest = rest - part.astype(F32)

    return pl.pallas_call(
        kernel,
        in_specs=[VMEM] * (len(parts) + 1),
        out_specs=VMEM,
        out_shape=jax.ShapeDtypeStruct((2, rows + 8, width), BF16),
        name="text_chunk",
    )(*parts, gains)


def text_whole(place, blocks, text_count):
    chunks, _, padded, width = blocks[0].shape
    rows = padded - 8

    def kernel(place_ref, b0, b1, b2, b3, key_ref, value_ref, gain_ref):
        gains = jnp.zeros((2, 128), F32)
        for j, ref in enumerate((b0, b1, b2, b3)):
            start = pl.multiple_of((place_ref[0] ^ j) * width, 128)
            for d in range(chunks):
                at = pl.multiple_of(lax.rem(place_ref[1] + (chunks - d), chunks) * rows, 8)
                key_ref[pl.ds(at, rows), pl.ds(start, width)] = ref[d, 0, :rows].astype(F32)
                value_ref[pl.ds(at, rows), pl.ds(start, width)] = ref[d, 1, :rows].astype(F32)
                tail = ref[d, 0, rows:, :128].astype(F32)
                gains = gains + (tail[0:2] + tail[2:4] + tail[4:6])
        gain_ref[...] = gains

    return pl.pallas_call(
        kernel,
        grid_spec=pltpu.PrefetchScalarGridSpec(
            num_scalar_prefetch=1, grid=(), in_specs=[VMEM] * 4, out_specs=[VMEM] * 3
        ),
        out_shape=[jax.ShapeDtypeStruct((text_count, 4 * width), F32)] * 2 + [jax.ShapeDtypeStruct((2, 128), F32)],
        name="text_whole",
    )(place, *blocks)


def local(queries, keys, values, text_keys, text_values, gain_q, gain_k, window_ext, text_len, out_grad):
    head_count = window_ext.shape[0]
    frames, half, columns, features = queries.shape[1:]
    text_count = text_keys.shape[1]
    peers, heights = lax.axis_size("tm"), lax.axis_size("height")
    quads = peers // 2
    assert frames == TILE_F and heights == 2 and peers % 2 == 0
    assert features == 128 * head_count and head_count == 12
    assert half % TILE_H == 0 and columns % TILE_W == 0 and text_count % (8 * quads) == 0
    axes = ("tm", "height")
    me = lax.axis_index("tm")
    quad = me // 2
    member = (me % 2) * 2 + lax.axis_index("height")
    place = jnp.stack([member, quad, jnp.full_like(quad, quads - 1)]).astype(jnp.int32)

    def swap(x, j):
        return lax.ppermute(x, axes, [(4 * n + m, 4 * n + (m ^ j)) for n in range(quads) for m in range(4)])

    def move(x, step):
        pairs = [(4 * n + m, 4 * (n + step(m // 2)) + m) for n in range(quads) for m in range(4)]
        return lax.ppermute(x, axes, [(i, j) for i, j in pairs if 0 <= j < 4 * quads])

    def turn(x, d):
        return lax.ppermute(x, axes, [(4 * n + m, 4 * ((n + d) % quads) + m) for n in range(quads) for m in range(4)])

    out_a, out_b = (lambda a: 2 * a - 1), (lambda a: 1 - 2 * a)
    flat = [x.reshape(-1, features) for x in (queries, keys, values, out_grad)]
    q, k, v, d = flat
    gq, gk = gain_q.reshape(1, -1), gain_k.reshape(1, -1)

    kv = pack(place, [k, v], [(2, (0, 1)), (3, (0, 1))])
    kv_in = [swap(kv[0], 2), swap(kv[1], 3)]
    near0, near1, qd2, qd3 = pack(place, [k, v, q, d], [(0, (0, 1, 2, 3)), (1, (0, 1, 2, 3)), (2, (2, 3)), (3, (2, 3))])
    near1 = swap(near1, 1)
    half_a = move(near0, out_a)
    qd_in = [swap(qd2, 2), swap(qd3, 3)]
    halos_a = [half_a, move(near1, out_a)]
    kv_halos = [move(x, out_b) for x in kv_in]
    qd_halos = [move(x, out_b) for x in qd_in]

    oq0, oq1, oq2, oq3, own, stats0, stats1, gain_part, *texts = attention(
        place, window_ext, text_len, flat, near1, kv_in, qd_in, halos_a + kv_halos,
        text_keys[0], text_values[0], gq, gk, (half, columns, quads),
    )
    after = move(stats0, lambda a: -1)
    before = move(stats1, lambda a: 1)
    text_in = [turn(texts[i], i) for i in range(1, quads)]
    oq_in = [swap(x, j) for x, j in zip((oq1, oq2, oq3), (1, 2, 3))]
    e0, e1, e2, e3, gains = edges(
        place, window_ext, own, (before, after), k, v, near1, kv_in, halos_a + qd_halos, gq, gk, gain_part, (half, columns)
    )
    gains = lax.psum(gains, "dp")
    ends_in = [swap(x, j) for x, j in zip((e1, e2, e3), (1, 2, 3))]
    chunk = text_chunk([texts[0]] + text_in, gains)
    block0 = jnp.stack([chunk] + [turn(chunk, i) for i in range(1, quads)])
    block1, block2 = swap(block0, 1), swap(block0, 2)
    block3 = swap(block2, 1)
    query_out = unpack(place, [oq0] + oq_in, BF16)[0]
    key_out, value_out = unpack(place, [e0] + ends_in, BF16)
    text_key_out, text_value_out, gain_out = text_whole(place, [block0, block1, block2, block3], text_count)
    shape = queries.shape
    return (
        query_out.reshape(shape),
        key_out.reshape(shape),
        value_out.reshape(shape),
        text_key_out[None],
        text_value_out[None],
        gain_out,
    )


def solution(mesh):
    tokens = P("dp", "tm", "height", None, None)
    words = P("dp", None, None)
    return jax.shard_map(
        local,
        mesh=mesh,
        in_specs=(tokens, tokens, tokens, words, words, P(), P(), P(), P("dp"), tokens),
        out_specs=(tokens, tokens, tokens, words, words, P()),
        check_vma=False,
    )
```

```python
import jax
import jax.numpy as jnp
from jax import lax
from jax.experimental import pallas as pl
from jax.experimental.pallas import tpu as pltpu
from jax.sharding import PartitionSpec as P


TILE_F = 2
TILE_H = 4
TILE_W = 4
EPS = 1e-06
HIDDEN = -1e30
LOG2E = 1.4426950408889634


VMEM = pl.BlockSpec(memory_space=pltpu.VMEM)
F32 = jnp.float32
BF16 = jnp.bfloat16


def dot(x, y, dims):
    return lax.dot_general(x, y, ((dims[:1], dims[1:]), ((), ())), preferred_element_type=F32)


def pack(place, arrays, groups):
    tokens, features = arrays[0].shape
    width = features // 4

    def kernel(place_ref, *refs):
        for out_ref, (j, picked) in zip(refs[len(arrays):], groups):
            start = pl.multiple_of((place_ref[0] ^ j) * width, 128)
            for i, n in enumerate(picked):
                out_ref[i] = refs[n][:, pl.ds(start, width)]

    return pl.pallas_call(
        kernel,
        grid_spec=pltpu.PrefetchScalarGridSpec(
            num_scalar_prefetch=1, grid=(), in_specs=[VMEM] * len(arrays), out_specs=[VMEM] * len(groups)
        ),
        out_shape=[jax.ShapeDtypeStruct((len(picked), tokens, width), arrays[0].dtype) for _, picked in groups],
        name="pack",
    )(place, *arrays)


def unpack(place, pieces, dtype):
    count, rows, width = pieces[0].shape

    def kernel(place_ref, *refs):
        for j in range(4):
            start = pl.multiple_of((place_ref[0] ^ j) * width, 128)
            for i in range(count):
                refs[4 + i][:, pl.ds(start, width)] = refs[j][i].astype(dtype)

    return pl.pallas_call(
        kernel,
        grid_spec=pltpu.PrefetchScalarGridSpec(
            num_scalar_prefetch=1, grid=(), in_specs=[VMEM] * 4, out_specs=[VMEM] * count
        ),
        out_shape=[jax.ShapeDtypeStruct((rows, 4 * width), dtype)] * count,
        name="unpack",
    )(place, *pieces)


def unit(x):
    x = x.astype(F32)
    inverse = lax.rsqrt(jnp.mean(x * x, axis=-1, keepdims=True) + EPS)
    return x * inverse, inverse


def spatial(half, columns, slot, ext1, ext2):
    shape = (2 * slot, 128)
    tile_rows, tile_cols = half // TILE_H, columns // TILE_W
    n = lax.broadcasted_iota(jnp.int32, shape, 0)
    row = (n // slot) * tile_rows + ((n // columns) % half) // TILE_H
    col = (n % columns) // TILE_W
    lane = lax.broadcasted_iota(jnp.int32, shape, 1)
    space = 2 * tile_rows * tile_cols
    code = lane % space
    near = (jnp.abs(row - code // tile_cols) <= ext1) & (jnp.abs(col - code % tile_cols) <= ext2)
    return near, lane, row * tile_cols + col, space


def hidden(seen):
    return jnp.where(seen, 0.0, HIDDEN).astype(BF16)


def attention_kernel(half, columns, slot, text_count, chunks, scale):
    tile = 2 * slot
    video = 4 * tile
    chunk = text_count // chunks

    def kernel(place_ref, ext_ref, len_ref, *refs):
        q0, k0, v0, d0, near1, kv2, kv3, qd1, qd2, qd3, ha0, ha1, hb0, hb1, tk, tv, gq_ref, gk_ref = refs[:18]
        oq0, oq1, oq2, oq3, own, stats0, stats1, ogain = refs[18:26]
        texts = refs[26:26 + chunks]
        kn, vs, qn, grads, qx, qr, dk, dv, oq = refs[26 + chunks:]
        h = pl.program_id(0)
        g, p, last = place_ref[0], place_ref[1], place_ref[2]
        a, b = g >> 1, g & 1
        head = 3 * g + h
        e0, e1, e2 = ext_ref[head, 0], ext_ref[head, 1], ext_ref[head, 2]
        gq, gk = gq_ref[...], gk_ref[...]
        spot = lambda start: pl.ds(pl.multiple_of(start, slot), slot)
        own_at = [(g ^ j) * slot for j in range(4)]
        a_base = jnp.where(a == 0, 3 * tile, 0)
        b_base = jnp.where(a == 0, 0, 3 * tile)
        halo_at = [a_base + b * slot, a_base + (1 - b) * slot, b_base + b * slot, b_base + (1 - b) * slot]

        key_parts = [(k0[...], v0[...])] + [(r[0], r[1]) for r in (near1, kv2, kv3)]
        key_parts = [(x, y, at + tile) for (x, y), at in zip(key_parts, own_at)]
        key_parts += [(r[0], r[1], at) for r, at in zip((ha0, ha1, hb0, hb1), halo_at)]
        for x, y, at in key_parts:
            kn[spot(at), :128] = (unit(x)[0] * gk).astype(BF16)
            vs[spot(at), :] = y
        kn[video:, :128] = tk[...]
        vs[video:, :] = tv[...]
        for (x, y), at in zip([(q0[...], d0[...])] + [(r[0], r[1]) for r in (qd1, qd2, qd3)], own_at):
            hat, inverse = unit(x)
            qx[spot(at), :] = hat
            qr[spot(at), :] = jnp.broadcast_to(inverse, hat.shape)
            qn[spot(at), :128] = (hat * gq).astype(BF16)
            grads[spot(at), :] = y

        near, lane, code, space = spatial(half, columns, slot, e1, e2)

        @pl.when(h == 0)
        def _():
            for t in range(2):
                qn[t * tile:(t + 1) * tile, 128:] = jnp.where(lane == t * space + code, 1.0, 0.0).astype(BF16)

        for block in range(4):
            seen = near & (jnp.abs(block - 1 - lane // space) <= e0)
            if block == 0:
                seen = seen & (p > 0)
            if block == 3:
                seen = seen & (p < last)
            kn[block * tile:(block + 1) * tile, 128:] = hidden(seen)
        word = lax.broadcasted_iota(jnp.int32, (text_count, 128), 0)
        kn[video:, 128:] = hidden(word < len_ref[0])

        gain_q = jnp.zeros((1, 128), F32)
        for t, stats in enumerate((stats0, stats1)):
            parts = (slice(t * tile, (t + 3) * tile), slice(video, video + text_count))
            rows = slice(t * tile, (t + 1) * tile)
            query, grad = qn[rows, :], grads[rows, :]
            scores = [dot(kn[x, :], query, (1, 1)) for x in parts]
            top = jnp.maximum(*[jnp.max(s, axis=0, keepdims=True) for s in scores])
            powers = [jnp.exp2((s - top) * (scale * LOG2E)) for s in scores]
            share = 1.0 / sum(jnp.sum(e, axis=0, keepdims=True) for e in powers)
            probs = [e * share for e in powers]
            low = [x.astype(BF16) for x in probs]
            attn = sum(dot(vs[x, :], w, (0, 0)) for x, w in zip(parts, low))
            delta = jnp.sum(grad.astype(F32).T * attn, axis=0, keepdims=True)
            stats[...] = jnp.zeros_like(stats)
            stats[0, 0:1, :] = top
            stats[0, 1:2, :] = share
            stats[0, 2:3, :] = delta
            prob_grad = [dot(vs[x, :], grad, (1, 1)) for x in parts]
            score_grad = [(w * (y - delta)).astype(BF16) for w, y in zip(probs, prob_grad)]
            dqn = sum(dot(kn[x, :128], s, (0, 0)) for x, s in zip(parts, score_grad)).T * scale
            mine = slice((1 - t) * tile, (3 - t) * tile)
            for x, w, s in ((slice(0, 2 * tile), low[0][mine], score_grad[0][mine]), (slice(2 * tile, None), low[1], score_grad[1])):
                value_part = dot(w, grad, (1, 0))
                key_part = dot(s, query[:, :128], (1, 0)) * scale
                if t == 0:
                    dv[x, :] = value_part
                    dk[x, :] = key_part
                else:
                    dv[x, :] += value_part
                    dk[x, :] += key_part
            hat = qx[rows, :]
            weighted = dqn * gq
            inner = jnp.mean(weighted * hat, axis=-1, keepdims=True)
            oq[rows, :] = (qr[rows, :] * (weighted - hat * inner)).astype(BF16)
            gain_q = gain_q + jnp.sum(dqn * hat, axis=0, keepdims=True)

        @pl.when(h == 0)
        def _():
            ogain[...] = gain_q

        @pl.when(h > 0)
        def _():
            ogain[...] += gain_q

        for j, out in enumerate((oq0, oq1, oq2, oq3)):
            out[0] = oq[spot(own_at[j]), :]
        own[0] = dk[:2 * tile, :]
        own[1] = dv[:2 * tile, :]
        for d, out in enumerate(texts):
            start = pl.multiple_of(2 * tile + lax.rem(p + d, chunks) * chunk, 8)
            out[0] = dk[pl.ds(start, chunk), :]
            out[1] = dv[pl.ds(start, chunk), :]

    return kernel


def attention(place, window_ext, text_len, own, near1, kv_in, qd_in, halos, text_keys, text_values, gain_q, gain_k, dims):
    half, columns, chunks = dims
    slot, features = own[0].shape
    width = features // 4
    heads = width // 128
    text_count = text_keys.shape[0]
    tile = 2 * slot
    mine = pl.BlockSpec((slot, 128), lambda h, pr, er, lr: (0, pr[0] * heads + h))
    front = pl.BlockSpec((2, slot, 128), lambda h, pr, er, lr: (0, 0, h))
    back = pl.BlockSpec((2, slot, 128), lambda h, pr, er, lr: (1, 0, h))
    text = pl.BlockSpec((text_count, 128), lambda h, pr, er, lr: (0, pr[0] * heads + h))
    fixed = pl.BlockSpec((1, 128), lambda h, pr, er, lr: (0, 0))
    stats = pl.BlockSpec((1, 8, tile), lambda h, pr, er, lr: (h, 0, 0))
    s = jax.ShapeDtypeStruct
    return pl.pallas_call(
        attention_kernel(half, columns, slot, text_count, chunks, 128 ** -0.5),
        grid_spec=pltpu.PrefetchScalarGridSpec(
            num_scalar_prefetch=3,
            grid=(heads,),
            in_specs=[mine] * 4 + [front] * 3 + [back] + [front] * 6 + [text] * 2 + [fixed] * 2,
            out_specs=[front_of(slot)] * 4
            + [pl.BlockSpec((2, 2 * tile, 128), lambda h, pr, er, lr: (0, 0, h)), stats, stats, fixed]
            + [pl.BlockSpec((2, text_count // chunks, 128), lambda h, pr, er, lr: (0, 0, h))] * chunks,
            scratch_shapes=[
                pltpu.VMEM((4 * tile + text_count, 256), BF16),
                pltpu.VMEM((4 * tile + text_count, 128), BF16),
                pltpu.VMEM((2 * tile, 256), BF16),
                pltpu.VMEM((2 * tile, 128), BF16),
                pltpu.VMEM((2 * tile, 128), F32),
                pltpu.VMEM((2 * tile, 128), F32),
                pltpu.VMEM((2 * tile + text_count, 128), F32),
                pltpu.VMEM((2 * tile + text_count, 128), F32),
                pltpu.VMEM((2 * tile, 128), BF16),
            ],
        ),
        out_shape=[s((1, slot, width), BF16)] * 4
        + [s((2, 2 * tile, width), F32), s((heads, 8, tile), F32), s((heads, 8, tile), F32), s((1, 128), F32)]
        + [s((2, text_count // chunks, width), F32)] * chunks,
        name="attention",
    )(place, window_ext, text_len, *own, near1, *kv_in, near1, *qd_in, *halos, text_keys, text_values, gain_q, gain_k)


def front_of(slot):
    return pl.BlockSpec((1, slot, 128), lambda h, pr, er, lr: (0, 0, h))


def edges(place, window_ext, own, stats, k, v, near1, kv_in, halos, gain_q, gain_k, gain_in, dims):
    half, columns = dims
    slot, features = k.shape
    width = features // 4
    heads = width // 128
    tile = 2 * slot
    scale = 128 ** -0.5

    def kernel(
        place_ref, ext_ref, own_ref, before_ref, after_ref, k0, v0, kv1, kv2, kv3, ha0, ha1, hb0, hb1,
        gq_ref, gk_ref, gain_ref, o0, o1, o2, o3, ogain, kn, vs, kx, kr, qn, grads, ends,
    ):
        h = pl.program_id(0)
        g, p, last = place_ref[0], place_ref[1], place_ref[2]
        a, b = g >> 1, g & 1
        head = 3 * g + h
        e0, e1, e2 = ext_ref[head, 0], ext_ref[head, 1], ext_ref[head, 2]
        gq, gk = gq_ref[...], gk_ref[...]
        spot = lambda start: pl.ds(pl.multiple_of(start, slot), slot)
        own_at = [(g ^ j) * slot for j in range(4)]
        a_base, b_base = (1 - a) * tile, a * tile
        halo_at = [a_base + b * slot, a_base + (1 - b) * slot, b_base + b * slot, b_base + (1 - b) * slot]
        for (x, y), at in zip([(k0[...], v0[...])] + [(r[0], r[1]) for r in (kv1, kv2, kv3)], own_at):
            hat, inverse = unit(x)
            kx[spot(at), :] = hat
            kr[spot(at), :] = jnp.broadcast_to(inverse, hat.shape)
            kn[spot(at), :128] = (hat * gk).astype(BF16)
            vs[spot(at), :] = y
        for r, at in zip((ha0, ha1, hb0, hb1), halo_at):
            qn[spot(at), :128] = (unit(r[0])[0] * gq).astype(BF16)
            grads[spot(at), :] = r[1]
        near, lane, code, _ = spatial(half, columns, slot, e1, e2)
        near = near & (e0 >= 1)
        for t in range(2):
            kn[t * tile:(t + 1) * tile, 128:] = hidden(near & ((p > 0) if t == 0 else (p < last)))

        @pl.when(h == 0)
        def _():
            for t in range(2):
                qn[t * tile:(t + 1) * tile, 128:] = jnp.where(lane == code, 1.0, 0.0).astype(BF16)

        gain_k = jnp.zeros((1, 128), F32)
        for t, stats_ref in enumerate((before_ref, after_ref)):
            rows = slice(t * tile, (t + 1) * tile)
            top, share, delta = stats_ref[0, 0:1, :], stats_ref[0, 1:2, :], stats_ref[0, 2:3, :]
            query, grad = qn[rows, :], grads[rows, :]
            probs = jnp.exp2((dot(kn[rows, :], query, (1, 1)) - top) * (scale * LOG2E)) * share
            prob_grad = dot(vs[rows, :], grad, (1, 1))
            score_grad = (probs * (prob_grad - delta)).astype(BF16)
            value_sum = own_ref[1, rows, :] + dot(probs.astype(BF16), grad, (1, 0))
            key_sum = own_ref[0, rows, :] + dot(score_grad, query[:, :128], (1, 0)) * scale
            hat = kx[rows, :]
            weighted = key_sum * gk
            inner = jnp.mean(weighted * hat, axis=-1, keepdims=True)
            ends[0, rows, :] = (kr[rows, :] * (weighted - hat * inner)).astype(BF16)
            ends[1, rows, :] = value_sum.astype(BF16)
            gain_k = gain_k + jnp.sum(key_sum * hat, axis=0, keepdims=True)

        @pl.when(h == 0)
        def _():
            ogain[0:1, :] = gain_ref[...]
            ogain[1:2, :] = gain_k

        @pl.when(h > 0)
        def _():
            ogain[1:2, :] += gain_k

        for j, out in enumerate((o0, o1, o2, o3)):
            out[0] = ends[0, spot(own_at[j]), :]
            out[1] = ends[1, spot(own_at[j]), :]

    mine = pl.BlockSpec((slot, 128), lambda h, pr, er: (0, pr[0] * heads + h))
    front = pl.BlockSpec((2, slot, 128), lambda h, pr, er: (0, 0, h))
    back = pl.BlockSpec((2, slot, 128), lambda h, pr, er: (1, 0, h))
    fixed = pl.BlockSpec((1, 128), lambda h, pr, er: (0, 0))
    stat = pl.BlockSpec((1, 8, tile), lambda h, pr, er: (h, 0, 0))
    s = jax.ShapeDtypeStruct
    return pl.pallas_call(
        kernel,
        grid_spec=pltpu.PrefetchScalarGridSpec(
            num_scalar_prefetch=2,
            grid=(heads,),
            in_specs=[pl.BlockSpec((2, 2 * tile, 128), lambda h, pr, er: (0, 0, h)), stat, stat, mine, mine]
            + [front] * 3
            + [back] * 2
            + [front] * 2
            + [fixed] * 3,
            out_specs=[front] * 4 + [pl.BlockSpec((2, 128), lambda h, pr, er: (0, 0))],
            scratch_shapes=[
                pltpu.VMEM((2 * tile, 256), BF16),
                pltpu.VMEM((2 * tile, 128), BF16),
                pltpu.VMEM((2 * tile, 128), F32),
                pltpu.VMEM((2 * tile, 128), F32),
                pltpu.VMEM((2 * tile, 256), BF16),
                pltpu.VMEM((2 * tile, 128), BF16),
                pltpu.VMEM((2, 2 * tile, 128), BF16),
            ],
        ),
        out_shape=[s((2, slot, width), BF16)] * 4 + [s((2, 128), F32)],
        name="edges",
    )(place, window_ext, own, *stats, k, v, near1, *kv_in, *halos, gain_q, gain_k, gain_in)


def text_chunk(parts, gains):
    _, rows, width = parts[0].shape

    def kernel(*refs):
        out_ref = refs[-1]
        total = refs[0][...]
        for ref in refs[1:-2]:
            total = total + ref[...]
        out_ref[:, :rows, :] = total.astype(BF16)
        out_ref[:, rows:, :] = jnp.zeros((2, 8, width), BF16)
        rest = refs[-2][...]
        for i in range(3):
            part = rest.astype(BF16)
            out_ref[0, rows + 2 * i:rows + 2 * i + 2, :128] = part
            rest = rest - part.astype(F32)

    return pl.pallas_call(
        kernel,
        in_specs=[VMEM] * (len(parts) + 1),
        out_specs=VMEM,
        out_shape=jax.ShapeDtypeStruct((2, rows + 8, width), BF16),
        name="text_chunk",
    )(*parts, gains)


def text_columns(place, sides, members, rows, earlier=None):
    counts = [len(side) for side in sides]
    pieces = [x for side in sides for x in side]
    chunks = counts[0] if pieces[0].ndim == 3 else pieces[0].shape[0]
    width = pieces[0].shape[-1]
    shape = (rows * chunks, 4 * width)

    def kernel(place_ref, *refs):
        ins = refs[:len(pieces)]
        key_ref, value_ref, gain_ref, hold, sems = refs[len(refs) - 5:]
        gains = refs[len(pieces)][...] if earlier is not None else jnp.zeros((2, 128), F32)
        copies = []
        for n, j in enumerate(members):
            mine = ins[sum(counts[:n]):sum(counts[:n + 1])]
            for d in range(chunks):
                at = pl.multiple_of(lax.rem(place_ref[1] + (chunks - d), chunks) * rows, 8)
                piece = mine[d] if len(mine) == chunks and chunks > 1 else mine[0].at[d]
                for i in range(2):
                    hold[n, i, pl.ds(at, rows), :] = piece[i, :rows].astype(F32)
                tail = piece[0, rows:, :128].astype(F32)
                gains = gains + (tail[0:2] + tail[2:4] + tail[4:6])
            start = pl.multiple_of((place_ref[0] ^ j) * width, 128)
            for i, out in enumerate((key_ref, value_ref)):
                copies.append(pltpu.make_async_copy(hold.at[n, i], out.at[:, pl.ds(start, width)], sems.at[n, i]))
                copies[-1].start()
        gain_ref[...] = gains
        for copy in copies:
            copy.wait()

    hbm = pl.BlockSpec(memory_space=pl.ANY)
    more = [] if earlier is None else [earlier[2], earlier[0], earlier[1]]
    return pl.pallas_call(
        kernel,
        grid_spec=pltpu.PrefetchScalarGridSpec(
            num_scalar_prefetch=1,
            grid=(),
            in_specs=[VMEM] * len(pieces) + ([] if earlier is None else [VMEM, hbm, hbm]),
            out_specs=[hbm, hbm, VMEM],
            scratch_shapes=[pltpu.VMEM((2, 2, rows * chunks, width), F32), pltpu.SemaphoreType.DMA((2, 2))],
        ),
        out_shape=[jax.ShapeDtypeStruct(shape, F32)] * 2 + [jax.ShapeDtypeStruct((2, 128), F32)],
        input_output_aliases={} if earlier is None else {len(pieces) + 2: 0, len(pieces) + 3: 1},
        name="text_columns",
    )(place, *pieces, *more)


def local(queries, keys, values, text_keys, text_values, gain_q, gain_k, window_ext, text_len, out_grad):
    head_count = window_ext.shape[0]
    frames, half, columns, features = queries.shape[1:]
    text_count = text_keys.shape[1]
    peers, heights = lax.axis_size("tm"), lax.axis_size("height")
    quads = peers // 2
    assert frames == TILE_F and heights == 2 and peers % 2 == 0
    assert features == 128 * head_count and head_count == 12
    assert half % TILE_H == 0 and columns % TILE_W == 0 and text_count % (8 * quads) == 0
    axes = ("tm", "height")
    me = lax.axis_index("tm")
    quad = me // 2
    member = (me % 2) * 2 + lax.axis_index("height")
    place = jnp.stack([member, quad, jnp.full_like(quad, quads - 1)]).astype(jnp.int32)

    def permute(x, pairs):
        return lax.ppermute(x, axes, pairs)

    def swap(x, j):
        return permute(x, [(4 * n + m, 4 * n + (m ^ j)) for n in range(quads) for m in range(4)])

    def move(x, step):
        pairs = [(4 * n + m, 4 * (n + step(m // 2)) + m) for n in range(quads) for m in range(4)]
        return permute(x, [(i, j) for i, j in pairs if 0 <= j < 4 * quads])

    def turn(x, d):
        return permute(x, [(4 * n + m, 4 * ((n + d) % quads) + m) for n in range(quads) for m in range(4)])

    out_a, out_b = (lambda a: 2 * a - 1), (lambda a: 1 - 2 * a)
    flat = [x.reshape(-1, features) for x in (queries, keys, values, out_grad)]
    q, k, v, d = flat
    gq, gk = gain_q.reshape(1, -1), gain_k.reshape(1, -1)

    kv = pack(place, [k, v], [(2, (0, 1)), (3, (0, 1))])
    kv_in = [swap(kv[0], 2), swap(kv[1], 3)]
    near0, near1, qd2, qd3 = pack(place, [k, v, q, d], [(0, (0, 1, 2, 3)), (1, (0, 1, 2, 3)), (2, (2, 3)), (3, (2, 3))])
    near1 = swap(near1, 1)
    halos_a = [move(near0, out_a), move(near1, out_a)]
    kv_halos = [move(kv_in[0], out_b), move(kv_in[1], out_b)]
    qd_in = [swap(qd2, 2), swap(qd3, 3)]
    qd_halos = [move(qd_in[0], out_b), move(qd_in[1], out_b)]

    oq0, oq1, oq2, oq3, own, stats0, stats1, gain_part, *texts = attention(
        place, window_ext, text_len, flat, near1, kv_in, qd_in, halos_a + kv_halos,
        text_keys[0], text_values[0], gq, gk, (half, columns, quads),
    )
    after = move(stats0, lambda a: -1)
    before = move(stats1, lambda a: 1)
    text_in = [turn(texts[i], i) for i in range(1, quads)]
    oq_in = [swap(x, j) for x, j in zip((oq1, oq2, oq3), (1, 2, 3))]
    e0, e1, e2, e3, gains = edges(
        place, window_ext, own, (before, after), k, v, near1, kv_in, halos_a + qd_halos, gq, gk, gain_part, (half, columns)
    )
    ends_in = [swap(x, j) for x, j in zip((e1, e2, e3), (1, 2, 3))]
    gains = lax.psum(gains, "dp")
    chunk = text_chunk([texts[0]] + text_in, gains)
    side0 = [chunk] + [turn(chunk, i) for i in range(1, quads)]
    side2 = [swap(x, 2) for x in side0]
    side1 = swap(jnp.stack(side0), 1)
    side3 = swap(jnp.stack(side2), 1)
    query_out = unpack(place, [oq0] + oq_in, BF16)[0]
    key_out, value_out = unpack(place, [e0] + ends_in, BF16)
    rows = text_count // quads
    early = text_columns(place, [side0, [side1]], (0, 1), rows)
    text_key_out, text_value_out, gain_out = text_columns(place, [side2, [side3]], (2, 3), rows, early)
    shape = queries.shape
    return (
        query_out.reshape(shape),
        key_out.reshape(shape),
        value_out.reshape(shape),
        text_key_out[None],
        text_value_out[None],
        gain_out,
    )


def solution(mesh):
    tokens = P("dp", "tm", "height", None, None)
    words = P("dp", None, None)

    return jax.shard_map(
        local,
        mesh=mesh,
        in_specs=(tokens, tokens, tokens, words, words, P(), P(), P(), P("dp"), tokens),
        out_specs=(tokens, tokens, tokens, words, words, P()),
        check_vma=False,
    )
```

```python
import jax
import jax.numpy as jnp
import numpy as np
from jax import lax
from jax.experimental import pallas as pl
from jax.experimental.pallas import tpu as pltpu
from jax.sharding import PartitionSpec as P


TILE_F = 2
TILE_H = 4
TILE_W = 4
EPS = 1e-06
HIDDEN = -1e30
LOG2E = 1.4426950408889634


F32 = jnp.float32
BF16 = jnp.bfloat16
VMEM = pl.BlockSpec(memory_space=pltpu.VMEM)
HBM = pl.BlockSpec(memory_space=pltpu.HBM)


def call(kernel, scalars, operands, outputs, scratch=(), aliases=None, limit=24):
    spec = {"vmem": VMEM, "hbm": HBM, "out": VMEM}
    held = [pltpu.with_memory_space_constraint(x, pltpu.VMEM) if space == "vmem" else x for x, space in operands]
    return pl.pallas_call(
        kernel,
        grid_spec=pltpu.PrefetchScalarGridSpec(
            num_scalar_prefetch=len(scalars),
            grid=(),
            in_specs=[spec[space] for _, space in operands],
            out_specs=[spec[space] for _, _, space in outputs],
            scratch_shapes=list(scratch),
        ),
        out_shape=[
            pltpu.VMEM(shape, dtype) if space == "vmem" else jax.ShapeDtypeStruct(shape, dtype)
            for shape, dtype, space in outputs
        ],
        input_output_aliases=aliases or {},
        compiler_params=pltpu.CompilerParams(vmem_limit_bytes=limit << 20),
    )(*scalars, *held)


def dot(x, y, dims):
    return lax.dot_general(x, y, ((dims[:1], dims[1:]), ((), ())), preferred_element_type=F32)


def pack(place, arrays, groups):
    tokens, features = arrays[0].shape
    width = features // 4
    total = sum(len(picked) for _, picked in groups)

    def kernel(place_ref, *refs):
        sems = refs[-1]
        copies = []
        for out_ref, (j, picked) in zip(refs[len(arrays):-1], groups):
            start = pl.multiple_of((place_ref[0] ^ j) * width, 128)
            for i, n in enumerate(picked):
                copies.append(
                    pltpu.make_async_copy(refs[n].at[:, pl.ds(start, width)], out_ref.at[i], sems.at[len(copies)])
                )
        for copy in copies:
            copy.start()
        for copy in copies:
            copy.wait()

    return call(
        kernel, [place], [(x, "hbm") for x in arrays],
        [((len(picked), tokens, width), arrays[0].dtype, "vmem") for _, picked in groups],
        [pltpu.SemaphoreType.DMA((total,))],
    )


def stage(place, texts, gains, masks):
    rows, features = texts[0].shape
    width = features // 4

    def kernel(place_ref, tk, tv, gq, gk, mask, text_ref, gain_ref, mask_ref, sems):
        columns = pl.ds(pl.multiple_of(place_ref[0] * width, 128), width)
        pairs = [(tk.at[:, columns], text_ref.at[0]), (tv.at[:, columns], text_ref.at[1])]
        pairs += [(gq, gain_ref.at[0:1]), (gk, gain_ref.at[1:2]), (mask, mask_ref)]
        copies = [pltpu.make_async_copy(x, y, sems.at[i]) for i, (x, y) in enumerate(pairs)]
        for copy in copies:
            copy.start()
        for copy in copies:
            copy.wait()

    return call(
        kernel, [place], [(x, "hbm") for x in (*texts, *gains, masks)],
        [((2, rows, width), texts[0].dtype, "vmem"), ((2, 128), F32, "vmem"), (masks.shape, F32, "vmem")],
        [pltpu.SemaphoreType.DMA((5,))],
    )


def unpack(place, pieces):
    count, rows, width = pieces[0].shape

    def kernel(place_ref, *refs):
        sems = refs[-1]
        copies = []
        for j in range(4):
            start = pl.multiple_of((place_ref[0] ^ j) * width, 128)
            for i in range(count):
                copies.append(
                    pltpu.make_async_copy(refs[j].at[i], refs[4 + i].at[:, pl.ds(start, width)], sems.at[len(copies)])
                )
        for copy in copies:
            copy.start()
        for copy in copies:
            copy.wait()

    return call(
        kernel, [place], [(x, "vmem") for x in pieces],
        [((rows, 4 * width), pieces[0].dtype, "hbm")] * count,
        [pltpu.SemaphoreType.DMA((4 * count,))],
    )


def unit(x):
    x = x.astype(F32)
    inverse = lax.rsqrt(jnp.mean(x * x, axis=-1, keepdims=True) + EPS)
    return x * inverse, inverse


def spatial(half, columns, slot):
    tile_rows, tile_cols = half // TILE_H, columns // TILE_W
    n = np.arange(2 * slot)
    row = (n // slot) * tile_rows + ((n // columns) % half) // TILE_H
    col = (n % columns) // TILE_W
    space = 2 * tile_rows * tile_cols
    code = np.arange(128) % space
    rows_off = np.abs(row[:, None] - code[None, :] // tile_cols)
    cols_off = np.abs(col[:, None] - code[None, :] % tile_cols)
    hot = ((row * tile_cols + col)[:, None] == np.arange(128)[None, :]) * 1.0
    return jnp.asarray(np.stack([rows_off, cols_off, hot]), F32), space


def hidden(seen):
    return jnp.where(seen, 0.0, HIDDEN).astype(BF16)


def spots(g, slot, near, far):
    a, b = g >> 1, g & 1
    a_base, b_base = jnp.where(a == 0, far, near), jnp.where(a == 0, near, far)
    halo = [a_base + b * slot, a_base + (1 - b) * slot, b_base + b * slot, b_base + (1 - b) * slot]
    return [(g ^ j) * slot for j in range(4)], halo


def attention(place, window_ext, text_len, near, kv, qd, halos, words, masks, space, gain, chunks):
    _, slot, width = near[0].shape
    heads = width // 128
    text_count = words.shape[1]
    tile = 2 * slot
    video = 4 * tile
    chunk = text_count // chunks
    scale = 128 ** -0.5

    def kernel(place_ref, ext_ref, len_ref, *refs):
        n0, n1, kv2, kv3, qd2, qd3, ha0, ha1, hb0, hb1, text_ref, mask_ref, gain_ref = refs[:13]
        oqs, own, ogain = refs[13:17], refs[17], refs[18]
        messages = refs[19:19 + chunks]
        kn, vs, kx, qn, grads, qx, qr, dk, dv, ends = refs[19 + chunks:]
        g, p, last = place_ref[0], place_ref[1], place_ref[2]
        gq, gk = gain_ref[0:1, :], gain_ref[1:2, :]
        at = lambda start: pl.ds(pl.multiple_of(start, slot), slot)
        own_at, halo_at = spots(g, slot, 0, 3 * tile)
        for t in range(2):
            hot = mask_ref[2] if t == 0 else pltpu.roll(mask_ref[2], space, 1)
            qn[t * tile:(t + 1) * tile, 128:] = hot.astype(BF16)
        lane_tile = lax.broadcasted_iota(jnp.int32, (1, 128), 1) // space
        word = lax.broadcasted_iota(jnp.int32, (text_count, 128), 0)
        kn[video:, 128:] = hidden(word < len_ref[0])
        ogain[...] = jnp.zeros((2, 128), F32)
        for out in messages:
            out[2 * chunk:, :] = jnp.zeros((8, width), F32)

        def one_head(h, _):
            lanes = pl.ds(pl.multiple_of(h * 128, 128), 128)
            head = heads * g + h
            e0, e1, e2 = ext_ref[0, head], ext_ref[1, head].astype(F32), ext_ref[2, head].astype(F32)

            sources = [(r, start + tile) for r, start in zip((n0, n1, kv2, kv3), own_at)]
            sources += list(zip((ha0, ha1, hb0, hb1), halo_at))
            for r, start in sources:
                hat, _ = unit(r[0, :, lanes])
                kx[at(start), :] = hat
                kn[at(start), :128] = (hat * gk).astype(BF16)
                vs[at(start), :] = r[1, :, lanes]
            kn[video:, :128] = text_ref[0, :, lanes]
            vs[video:, :] = text_ref[1, :, lanes]
            for r, i, start in zip((n0, n1, qd2, qd3), (2, 2, 0, 0), own_at):
                hat, inverse = unit(r[i, :, lanes])
                qx[at(start), :] = hat
                qr[at(start), :] = jnp.broadcast_to(inverse, hat.shape)
                qn[at(start), :128] = (hat * gq).astype(BF16)
                grads[at(start), :] = r[i + 1, :, lanes]
            close = (mask_ref[0] <= e1) & (mask_ref[1] <= e2)
            for block in range(4):
                framed = jnp.abs(block - 1 - lane_tile) <= e0
                if block == 0:
                    framed = framed & (p > 0)
                if block == 3:
                    framed = framed & (p < last)
                kn[block * tile:(block + 1) * tile, 128:] = hidden(close & framed)

            words = slice(video, video + text_count)
            parts = [(slice(t * tile, (t + 3) * tile), words) for t in range(2)]
            rows = [slice(t * tile, (t + 1) * tile) for t in range(2)]

            def softmax(scores):
                top = jnp.maximum(*[jnp.max(s, axis=0, keepdims=True) for s in scores])
                powers = [jnp.exp2((s - top) * (scale * LOG2E)) for s in scores]
                share = 1.0 / sum(jnp.sum(e, axis=0, keepdims=True) for e in powers)
                probs = [e * share for e in powers]
                return top, share, probs, [x.astype(BF16) for x in probs]

            scores = [[dot(kn[x, :], qn[rows[t], :], (1, 1)) for x in parts[t]] for t in range(2)]
            soft = [softmax(scores[t]) for t in range(2)]
            for t in range(2):
                top, share, probs, low = soft[t]
                query, grad = qn[rows[t], :128], grads[rows[t], :]
                attn = sum(dot(vs[x, :], w, (0, 0)) for x, w in zip(parts[t], low))
                prob_grad = [dot(vs[x, :], grad, (1, 1)) for x in parts[t]]
                delta = jnp.sum(grad.astype(F32).T * attn, axis=0, keepdims=True)
                message = messages[chunks - 1] if t == 0 else messages[1]
                for i, number in enumerate((top, share, delta)):
                    for side in range(2):
                        row = 2 * chunk + 2 * i + side
                        message[row:row + 1, lanes] = number[:, side * 128:side * 128 + 128]
                score_grad = [(w * (y - delta)).astype(BF16) for w, y in zip(probs, prob_grad)]
                dqn = sum(dot(kn[x, :128], s, (0, 0)) for x, s in zip(parts[t], score_grad)).T * scale
                mine = slice((1 - t) * tile, (3 - t) * tile)
                for x, w, s in (
                    (slice(0, 2 * tile), low[0][mine], score_grad[0][mine]),
                    (slice(2 * tile, 2 * tile + text_count), low[1], score_grad[1]),
                ):
                    value_part = dot(w, grad, (1, 0))
                    key_part = dot(s, query, (1, 0)) * scale
                    if t == 0:
                        dv[x, :] = value_part
                        dk[x, :] = key_part
                    else:
                        dv[x, :] += value_part
                        dk[x, :] += key_part
                hat = qx[rows[t], :]
                weighted = dqn * gq
                inner = jnp.mean(weighted * hat, axis=-1, keepdims=True)
                ends[rows[t], :] = (qr[rows[t], :] * (weighted - hat * inner)).astype(BF16)
                ogain[0:1, :] += jnp.sum(dqn * hat, axis=0, keepdims=True)
                around = slice(2 * t * tile, (2 * t + 1) * tile)
                key_part = dot(score_grad[0][around], query, (1, 0)) * scale
                where = slice(3 * t * tile, (3 * t + 1) * tile)
                ogain[1:2, :] += jnp.sum(key_part * kx[where, :], axis=0, keepdims=True)
            ogain[1:2, :] += jnp.sum(dk[:2 * tile, :] * kx[tile:3 * tile, :], axis=0, keepdims=True)

            for j, out in enumerate(oqs):
                out[0, :, lanes] = ends[at(own_at[j]), :]
            own[0, :, lanes] = dk[:2 * tile, :]
            own[1, :, lanes] = dv[:2 * tile, :]
            for d, out in enumerate(messages):
                start = pl.multiple_of(2 * tile + lax.rem(p + d, chunks) * chunk, 8)
                out[:chunk, lanes] = dk[pl.ds(start, chunk), :]
                out[chunk:2 * chunk, lanes] = dv[pl.ds(start, chunk), :]
            return 0

        lax.fori_loop(0, heads, one_head, 0)

    operands = [*near, *kv, *qd, *halos, words, masks, gain]
    return call(
        kernel, [place, window_ext, text_len], [(x, "vmem") for x in operands],
        [((1, slot, width), BF16, "vmem")] * 4
        + [((2, 2 * tile, width), F32, "vmem"), ((2, 128), F32, "vmem")]
        + [((2 * chunk + 8, width), F32, "vmem")] * chunks,
        [
            pltpu.VMEM((video + text_count, 256), BF16),
            pltpu.VMEM((video + text_count, 128), BF16),
            pltpu.VMEM((video, 128), F32),
            pltpu.VMEM((2 * tile, 256), BF16),
            pltpu.VMEM((2 * tile, 128), BF16),
            pltpu.VMEM((2 * tile, 128), F32),
            pltpu.VMEM((2 * tile, 128), F32),
            pltpu.VMEM((2 * tile + text_count, 128), F32),
            pltpu.VMEM((2 * tile + text_count, 128), F32),
            pltpu.VMEM((2 * tile, 128), BF16),
        ],
    )


def edges(place, window_ext, own, messages, near, kv, halos_a, halos_b, masks, gain):
    _, slot, width = near[0].shape
    heads = width // 128
    tile = 2 * slot
    chunk = (messages[0].shape[0] - 8) // 2
    scale = 128 ** -0.5

    def kernel(place_ref, ext_ref, *refs):
        own_ref, before_ref, after_ref, n0, n1, kv2, kv3, ha0, ha1, hb0, hb1 = refs[:11]
        mask_ref, gain_ref, o0, o1, o2, o3 = refs[11:17]
        kn, vs, kx, kr, qn, grads, ends = refs[17:]
        g, p, last = place_ref[0], place_ref[1], place_ref[2]
        gq, gk = gain_ref[0:1, :], gain_ref[1:2, :]
        at = lambda start: pl.ds(pl.multiple_of(start, slot), slot)
        own_at, halo_at = spots(g, slot, 0, tile)
        for t in range(2):
            qn[t * tile:(t + 1) * tile, 128:] = mask_ref[2].astype(BF16)

        def one_head(h, _):
            lanes = pl.ds(pl.multiple_of(h * 128, 128), 128)
            head = heads * g + h
            e0, e1, e2 = ext_ref[0, head], ext_ref[1, head].astype(F32), ext_ref[2, head].astype(F32)
            for r, start in zip((n0, n1, kv2, kv3), own_at):
                hat, inverse = unit(r[0, :, lanes])
                kx[at(start), :] = hat
                kr[at(start), :] = jnp.broadcast_to(inverse, hat.shape)
                kn[at(start), :128] = (hat * gk).astype(BF16)
                vs[at(start), :] = r[1, :, lanes]
            for r, i, start in zip((ha0, ha1, hb0, hb1), (2, 2, 0, 0), halo_at):
                qn[at(start), :128] = (unit(r[i, :, lanes])[0] * gq).astype(BF16)
                grads[at(start), :] = r[i + 1, :, lanes]
            close = (mask_ref[0] <= e1) & (mask_ref[1] <= e2) & (e0 >= 1)
            for t in range(2):
                kn[t * tile:(t + 1) * tile, 128:] = hidden(close & ((p > 0) if t == 0 else (p < last)))
            for t, message in enumerate((before_ref, after_ref)):
                rows = slice(t * tile, (t + 1) * tile)
                top, share, delta = [
                    jnp.concatenate([message[2 * chunk + i:2 * chunk + i + 1, lanes] for i in (n, n + 1)], axis=1)
                    for n in (0, 2, 4)
                ]
                query, grad = qn[rows, :], grads[rows, :]
                probs = jnp.exp2((dot(kn[rows, :], query, (1, 1)) - top) * (scale * LOG2E)) * share
                prob_grad = dot(vs[rows, :], grad, (1, 1))
                score_grad = (probs * (prob_grad - delta)).astype(BF16)
                value_sum = own_ref[1, rows, lanes] + dot(probs.astype(BF16), grad, (1, 0))
                key_sum = own_ref[0, rows, lanes] + dot(score_grad, query[:, :128], (1, 0)) * scale
                hat = kx[rows, :]
                weighted = key_sum * gk
                inner = jnp.mean(weighted * hat, axis=-1, keepdims=True)
                ends[0, rows, :] = (kr[rows, :] * (weighted - hat * inner)).astype(BF16)
                ends[1, rows, :] = value_sum.astype(BF16)
            for j, out in enumerate((o0, o1, o2, o3)):
                out[0, :, lanes] = ends[0, at(own_at[j]), :]
                out[1, :, lanes] = ends[1, at(own_at[j]), :]
            return 0

        lax.fori_loop(0, heads, one_head, 0)

    operands = [own, *messages, *near, *kv, *halos_a, *halos_b, masks, gain]
    return call(
        kernel, [place, window_ext], [(x, "vmem") for x in operands],
        [((2, slot, width), BF16, "vmem")] * 4,
        [
            pltpu.VMEM((2 * tile, 256), BF16),
            pltpu.VMEM((2 * tile, 128), BF16),
            pltpu.VMEM((2 * tile, 128), F32),
            pltpu.VMEM((2 * tile, 128), F32),
            pltpu.VMEM((2 * tile, 256), BF16),
            pltpu.VMEM((2 * tile, 128), BF16),
            pltpu.VMEM((2, 2 * tile, 128), BF16),
        ],
    )


def text_chunk(parts, gains):
    padded, width = parts[0].shape
    rows = padded - 8

    def kernel(*refs):
        sums, tails, out_ref = refs[:len(parts)], refs[len(parts):-1], refs[-1]
        total = sums[0][:rows, :]
        for ref in sums[1:]:
            total = total + ref[:rows, :]
        out_ref[:rows, :] = total.astype(BF16)
        out_ref[rows:, :] = jnp.zeros((8, width), BF16)
        rest = tails[0][...]
        for ref in tails[1:]:
            rest = rest + ref[...]
        for i in range(3):
            part = rest.astype(BF16)
            out_ref[rows + 2 * i:rows + 2 * i + 2, :128] = part
            rest = rest - part.astype(F32)

    return call(kernel, [], [(x, "vmem") for x in parts + gains], [((padded, width), BF16, "vmem")])[0]


def text_columns(place, members, firsts, rests, earlier=None):
    chunks, padded, width = rests[0].shape
    chunks, rows = chunks + 1, (padded - 8) // 2
    shape = (rows * chunks, 4 * width)

    def kernel(place_ref, *refs):
        key_ref, value_ref, gain_ref, hold, sems = refs[len(refs) - 5:]
        gains = refs[4][...] if earlier is not None else jnp.zeros((2, 128), F32)
        copies = []
        for n, j in enumerate(members):
            for d in range(chunks):
                piece = refs[n] if d == 0 else refs[2 + n].at[d - 1]
                start = pl.multiple_of(lax.rem(place_ref[1] + (chunks - d), chunks) * rows, 8)
                for i in range(2):
                    hold[n, i, pl.ds(start, rows), :] = piece[i * rows:(i + 1) * rows].astype(F32)
                tail = piece[2 * rows:, :128].astype(F32)
                gains = gains + (tail[0:2] + tail[2:4] + tail[4:6])
            start = pl.multiple_of((place_ref[0] ^ j) * width, 128)
            for i, out in enumerate((key_ref, value_ref)):
                copies.append(pltpu.make_async_copy(hold.at[n, i], out.at[:, pl.ds(start, width)], sems.at[n, i]))
                copies[-1].start()
        gain_ref[...] = gains
        for copy in copies:
            copy.wait()

    more = [] if earlier is None else [(earlier[2], "vmem"), (earlier[0], "hbm"), (earlier[1], "hbm")]
    return call(
        kernel, [place], [(x, "vmem") for x in (*firsts, *rests)] + more,
        [(shape, F32, "hbm"), (shape, F32, "hbm"), ((2, 128), F32, "vmem" if earlier is None else "out")],
        [pltpu.VMEM((2, 2, rows * chunks, width), F32), pltpu.SemaphoreType.DMA((2, 2))],
        {} if earlier is None else {6: 0, 7: 1},
    )


def local(queries, keys, values, text_keys, text_values, gain_q, gain_k, window_ext, text_len, out_grad):
    head_count = window_ext.shape[0]
    frames, half, columns, features = queries.shape[1:]
    text_count = text_keys.shape[1]
    peers, heights, samples = lax.axis_size("tm"), lax.axis_size("height"), lax.axis_size("dp")
    quads = peers // 2
    assert frames == TILE_F and heights == 2 and peers % 2 == 0 and quads >= 3
    assert features == 128 * head_count and head_count % 4 == 0
    assert half % TILE_H == 0 and columns % TILE_W == 0 and text_count % (8 * quads) == 0
    axes = ("tm", "height")
    me = lax.axis_index("tm")
    quad = me // 2
    member = (me % 2) * 2 + lax.axis_index("height")
    place = jnp.stack([member, quad, jnp.full_like(quad, quads - 1)]).astype(jnp.int32)

    def permute(x, pairs, over=axes):
        return lax.ppermute(x, over, pairs)

    def swap(x, j):
        return permute(x, [(4 * n + m, 4 * n + (m ^ j)) for n in range(quads) for m in range(4)])

    def move(x, step):
        pairs = [(4 * n + m, 4 * (n + step(m // 2)) + m) for n in range(quads) for m in range(4)]
        return permute(x, [(i, j) for i, j in pairs if 0 <= j < 4 * quads])

    def turn(x, d):
        return permute(x, [(4 * n + m, 4 * ((n + d) % quads) + m) for n in range(quads) for m in range(4)])

    out_a, out_b = (lambda a: 2 * a - 1), (lambda a: 1 - 2 * a)
    flat = [x.reshape(-1, features) for x in (keys, values, queries, out_grad)]
    table, space = spatial(half, columns, columns * half * frames)

    near0, near1, kv2, kv3, qd2, qd3 = pack(
        place, flat, [(0, (0, 1, 2, 3)), (1, (0, 1, 2, 3)), (2, (0, 1)), (3, (0, 1)), (2, (2, 3)), (3, (2, 3))]
    )
    kv_in = [swap(kv2, 2), swap(kv3, 3)]
    qd_in = [swap(qd2, 2), swap(qd3, 3)]
    words, gain, masks = stage(
        place, (text_keys[0], text_values[0]), (gain_q.reshape(1, -1), gain_k.reshape(1, -1)), table
    )
    near = [near0, swap(near1, 1)]
    halos_a = [move(near[0], out_a), move(near[1], out_a)]
    kv_halos = [move(kv_in[0], out_b), move(kv_in[1], out_b)]
    qd_halos = [move(qd_in[0], out_b), move(qd_in[1], out_b)]
    ext = window_ext.T

    oq0, oq1, oq2, oq3, own, gains, *texts = attention(
        place, ext, text_len, near, kv_in, qd_in, halos_a + kv_halos, words, masks, space, gain, quads
    )
    text_in = [turn(texts[i], i) for i in range(1, quads)]
    others = [permute(gains, [(n, (n + i) % samples) for n in range(samples)], "dp") for i in range(1, samples)]
    oq_in = [swap(x, j) for x, j in zip((oq1, oq2, oq3), (1, 2, 3))]
    (query_out,) = unpack(place, [oq0] + oq_in)
    chunk = text_chunk([texts[0]] + text_in, [gains] + others)
    rest = jnp.stack([turn(chunk, i) for i in range(1, quads)])
    across = swap(chunk, 2)
    side1 = swap(chunk, 1)
    side3 = swap(across, 1)
    ends = edges(place, ext, own, (text_in[0], text_in[-1]), near, kv_in, halos_a, qd_halos, masks, gain)
    ends_in = [swap(ends[j], j) for j in (1, 2, 3)]
    across_rest = swap(rest, 2)
    side1_rest = swap(rest, 1)
    side3_rest = swap(across_rest, 1)
    key_out, value_out = unpack(place, [ends[0]] + ends_in)
    early = text_columns(place, (0, 1), (chunk, side1), (rest, side1_rest))
    text_key_out, text_value_out, gain_out = text_columns(
        place, (2, 3), (across, side3), (across_rest, side3_rest), early
    )
    shape = queries.shape
    return (
        query_out.reshape(shape),
        key_out.reshape(shape),
        value_out.reshape(shape),
        text_key_out[None],
        text_value_out[None],
        gain_out,
    )


def solution(mesh):
    tokens = P("dp", "tm", "height", None, None)
    words = P("dp", None, None)

    return jax.shard_map(
        local,
        mesh=mesh,
        in_specs=(tokens, tokens, tokens, words, words, P(), P(), P(), P("dp"), tokens),
        out_specs=(tokens, tokens, tokens, words, words, P()),
        check_vma=False,
    )
```

```python
import jax
import jax.numpy as jnp
import numpy as np
from jax import lax
from jax.experimental import pallas as pl
from jax.experimental.pallas import tpu as pltpu
from jax.sharding import PartitionSpec as P


TILE_F = 2
TILE_H = 4
TILE_W = 4
EPS = 1e-06
HIDDEN = -1e30
LOG2E = 1.4426950408889634


F32 = jnp.float32
BF16 = jnp.bfloat16
VMEM = pl.BlockSpec(memory_space=pltpu.VMEM)
HBM = pl.BlockSpec(memory_space=pltpu.HBM)


def call(kernel, scalars, operands, outputs, scratch=(), aliases=None, limit=24):
    spec = {"vmem": VMEM, "hbm": HBM, "out": VMEM}
    spaces = {"vmem": pltpu.VMEM, "hbm": pltpu.HBM}
    held = [pltpu.with_memory_space_constraint(x, spaces[space]) for x, space in operands]
    return pl.pallas_call(
        kernel,
        grid_spec=pltpu.PrefetchScalarGridSpec(
            num_scalar_prefetch=len(scalars),
            grid=(),
            in_specs=[spec[space] for _, space in operands],
            out_specs=[spec[space] for _, _, space in outputs],
            scratch_shapes=list(scratch),
        ),
        out_shape=[
            pltpu.VMEM(shape, dtype) if space == "vmem" else jax.ShapeDtypeStruct(shape, dtype)
            for shape, dtype, space in outputs
        ],
        input_output_aliases=aliases or {},
        compiler_params=pltpu.CompilerParams(vmem_limit_bytes=limit << 20),
    )(*scalars, *held)


def dot(x, y, dims):
    return lax.dot_general(x, y, ((dims[:1], dims[1:]), ((), ())), preferred_element_type=F32)


def pack(place, arrays, groups):
    tokens, features = arrays[0].shape
    width = features // 4
    total = sum(len(picked) for _, picked in groups)

    def kernel(place_ref, *refs):
        sems = refs[-1]
        copies = []
        for out_ref, (j, picked) in zip(refs[len(arrays):-1], groups):
            start = pl.multiple_of((place_ref[0] ^ j) * width, 128)
            for i, n in enumerate(picked):
                copies.append(
                    pltpu.make_async_copy(refs[n].at[:, pl.ds(start, width)], out_ref.at[i], sems.at[len(copies)])
                )
        for copy in copies:
            copy.start()
        for copy in copies:
            copy.wait()

    return call(
        kernel, [place], [(x, "hbm") for x in arrays],
        [((len(picked), tokens, width), arrays[0].dtype, "vmem") for _, picked in groups],
        [pltpu.SemaphoreType.DMA((total,))],
    )


def stage(place, texts, gains, masks):
    rows, features = texts[0].shape
    width = features // 4

    def kernel(place_ref, tk, tv, gq, gk, mask, text_ref, gain_ref, mask_ref, sems):
        columns = pl.ds(pl.multiple_of(place_ref[0] * width, 128), width)
        pairs = [(tk.at[:, columns], text_ref.at[0]), (tv.at[:, columns], text_ref.at[1])]
        pairs += [(gq, gain_ref.at[0:1]), (gk, gain_ref.at[1:2]), (mask, mask_ref)]
        copies = [pltpu.make_async_copy(x, y, sems.at[i]) for i, (x, y) in enumerate(pairs)]
        for copy in copies:
            copy.start()
        for copy in copies:
            copy.wait()

    return call(
        kernel, [place], [(x, "hbm") for x in (*texts, *gains, masks)],
        [((2, rows, width), texts[0].dtype, "vmem"), ((2, 128), F32, "vmem"), (masks.shape, F32, "vmem")],
        [pltpu.SemaphoreType.DMA((5,))],
    )


def join(groups):
    arrays = []
    for group in groups:
        arrays += [x for x, _, _ in group if all(x is not y for y in arrays)]
    index = lambda x: [x is y for y in arrays].index(True)

    def kernel(*refs):
        for group, out in zip(groups, refs[len(arrays):]):
            for i, (x, first, last) in enumerate(group):
                out[i] = refs[index(x)][first:last]

    outputs = [((len(group), group[0][2] - group[0][1], *group[0][0].shape[1:]), arrays[0].dtype, "vmem") for group in groups]
    return call(kernel, [], [(x, "vmem") for x in arrays], outputs)


def unpack(place, pieces):
    count, rows, width = pieces[0].shape

    def kernel(place_ref, *refs):
        sems = refs[-1]
        copies = []
        for j in range(4):
            start = pl.multiple_of((place_ref[0] ^ j) * width, 128)
            for i in range(count):
                copies.append(
                    pltpu.make_async_copy(refs[j].at[i], refs[4 + i].at[:, pl.ds(start, width)], sems.at[len(copies)])
                )
        for copy in copies:
            copy.start()
        for copy in copies:
            copy.wait()

    return call(
        kernel, [place], [(x, "vmem") for x in pieces],
        [((rows, 4 * width), pieces[0].dtype, "hbm")] * count,
        [pltpu.SemaphoreType.DMA((4 * count,))],
    )


def unit(x):
    x = x.astype(F32)
    inverse = lax.rsqrt(jnp.mean(x * x, axis=-1, keepdims=True) + EPS)
    return x * inverse, inverse


def spatial(half, columns, slot):
    tile_rows, tile_cols = half // TILE_H, columns // TILE_W
    n = np.arange(2 * slot)
    row = (n // slot) * tile_rows + ((n // columns) % half) // TILE_H
    col = (n % columns) // TILE_W
    space = 2 * tile_rows * tile_cols
    code = np.arange(128) % space
    rows_off = np.abs(row[:, None] - code[None, :] // tile_cols)
    cols_off = np.abs(col[:, None] - code[None, :] % tile_cols)
    hot = ((row * tile_cols + col)[:, None] == np.arange(128)[None, :]) * 1.0
    return jnp.asarray(np.stack([rows_off, cols_off, hot]), F32), space


def hidden(seen):
    return jnp.where(seen, 0.0, HIDDEN).astype(BF16)


def spots(g, slot, near, far):
    a, b = g >> 1, g & 1
    a_base, b_base = jnp.where(a == 0, far, near), jnp.where(a == 0, near, far)
    halo = [a_base + b * slot, a_base + (1 - b) * slot, b_base + b * slot, b_base + (1 - b) * slot]
    return [(g ^ j) * slot for j in range(4)], halo


def attention(place, window_ext, text_len, near, kv, qd, halos, words, masks, space, gain, chunks):
    _, slot, width = near[0].shape
    heads = width // 128
    text_count = words.shape[1]
    tile = 2 * slot
    video = 4 * tile
    chunk = text_count // chunks
    scale = 128 ** -0.5

    def kernel(place_ref, ext_ref, len_ref, *refs):
        n0, n1, kv2, kv3, qd2, qd3, ha, hb, text_ref, mask_ref, gain_ref = refs[:11]
        oqs, own, ogain, stats = refs[11:15], refs[15], refs[16], refs[17:19]
        messages = refs[19:19 + chunks]
        kn, vs, kx, qn, grads, qx, qr, dk, dv, ends = refs[19 + chunks:]
        g, p, last = place_ref[0], place_ref[1], place_ref[2]
        gq, gk = gain_ref[0:1, :], gain_ref[1:2, :]
        at = lambda start: pl.ds(pl.multiple_of(start, slot), slot)
        own_at, halo_at = spots(g, slot, 0, 3 * tile)
        for t in range(2):
            hot = mask_ref[2] if t == 0 else pltpu.roll(mask_ref[2], space, 1)
            qn[t * tile:(t + 1) * tile, 128:] = hot.astype(BF16)
        lane_tile = lax.broadcasted_iota(jnp.int32, (1, 128), 1) // space
        word = lax.broadcasted_iota(jnp.int32, (text_count, 128), 0)
        kn[video:, 128:] = hidden(word < len_ref[0])
        ogain[...] = jnp.zeros((2, 128), F32)
        for out in stats:
            out[...] = jnp.zeros((8, width), F32)

        def one_head(h, _):
            lanes = pl.ds(pl.multiple_of(h * 128, 128), 128)
            head = heads * g + h
            e0, e1, e2 = ext_ref[0, head], ext_ref[1, head].astype(F32), ext_ref[2, head].astype(F32)

            sources = [(r, start + tile) for r, start in zip((n0, n1, kv2, kv3), own_at)]
            sources += list(zip((ha.at[0], ha.at[1], hb.at[0], hb.at[1]), halo_at))
            for r, start in sources:
                hat, _ = unit(r[0, :, lanes])
                kx[at(start), :] = hat
                kn[at(start), :128] = (hat * gk).astype(BF16)
                vs[at(start), :] = r[1, :, lanes]
            kn[video:, :128] = text_ref[0, :, lanes]
            vs[video:, :] = text_ref[1, :, lanes]
            for r, i, start in zip((n0, n1, qd2, qd3), (2, 2, 0, 0), own_at):
                hat, inverse = unit(r[i, :, lanes])
                qx[at(start), :] = hat
                qr[at(start), :] = jnp.broadcast_to(inverse, hat.shape)
                qn[at(start), :128] = (hat * gq).astype(BF16)
                grads[at(start), :] = r[i + 1, :, lanes]
            close = (mask_ref[0] <= e1) & (mask_ref[1] <= e2)
            for block in range(4):
                framed = jnp.abs(block - 1 - lane_tile) <= e0
                if block == 0:
                    framed = framed & (p > 0)
                if block == 3:
                    framed = framed & (p < last)
                kn[block * tile:(block + 1) * tile, 128:] = hidden(close & framed)

            words = slice(video, video + text_count)
            parts = [(slice(t * tile, (t + 3) * tile), words) for t in range(2)]
            rows = [slice(t * tile, (t + 1) * tile) for t in range(2)]

            def softmax(scores):
                top = jnp.maximum(*[jnp.max(s, axis=0, keepdims=True) for s in scores])
                powers = [jnp.exp2((s - top) * (scale * LOG2E)) for s in scores]
                share = 1.0 / sum(jnp.sum(e, axis=0, keepdims=True) for e in powers)
                probs = [e * share for e in powers]
                return top, share, probs, [x.astype(BF16) for x in probs]

            scores = [[dot(kn[x, :], qn[rows[t], :], (1, 1)) for x in parts[t]] for t in range(2)]
            soft = [softmax(scores[t]) for t in range(2)]
            for t in range(2):
                top, share, probs, low = soft[t]
                query, grad = qn[rows[t], :128], grads[rows[t], :]
                attn = sum(dot(vs[x, :], w, (0, 0)) for x, w in zip(parts[t], low))
                prob_grad = [dot(vs[x, :], grad, (1, 1)) for x in parts[t]]
                delta = jnp.sum(grad.astype(F32).T * attn, axis=0, keepdims=True)
                for i, number in enumerate((top, share, delta)):
                    for side in range(2):
                        row = 2 * i + side
                        stats[t][row:row + 1, lanes] = number[:, side * 128:side * 128 + 128]
                score_grad = [(w * (y - delta)).astype(BF16) for w, y in zip(probs, prob_grad)]
                dqn = sum(dot(kn[x, :128], s, (0, 0)) for x, s in zip(parts[t], score_grad)).T * scale
                mine = slice((1 - t) * tile, (3 - t) * tile)
                for x, w, s in (
                    (slice(0, 2 * tile), low[0][mine], score_grad[0][mine]),
                    (slice(2 * tile, 2 * tile + text_count), low[1], score_grad[1]),
                ):
                    value_part = dot(w, grad, (1, 0))
                    key_part = dot(s, query, (1, 0)) * scale
                    if t == 0:
                        dv[x, :] = value_part
                        dk[x, :] = key_part
                    else:
                        dv[x, :] += value_part
                        dk[x, :] += key_part
                hat = qx[rows[t], :]
                weighted = dqn * gq
                inner = jnp.mean(weighted * hat, axis=-1, keepdims=True)
                ends[rows[t], :] = (qr[rows[t], :] * (weighted - hat * inner)).astype(BF16)
                ogain[0:1, :] += jnp.sum(dqn * hat, axis=0, keepdims=True)
                around = slice(2 * t * tile, (2 * t + 1) * tile)
                key_part = dot(score_grad[0][around], query, (1, 0)) * scale
                where = slice(3 * t * tile, (3 * t + 1) * tile)
                ogain[1:2, :] += jnp.sum(key_part * kx[where, :], axis=0, keepdims=True)
            ogain[1:2, :] += jnp.sum(dk[:2 * tile, :] * kx[tile:3 * tile, :], axis=0, keepdims=True)

            for j, out in enumerate(oqs):
                out[0, :, lanes] = ends[at(own_at[j]), :]
            own[0, :, lanes] = dk[:2 * tile, :]
            own[1, :, lanes] = dv[:2 * tile, :]
            for d, out in enumerate(messages):
                start = pl.multiple_of(2 * tile + lax.rem(p + d, chunks) * chunk, 8)
                out[:chunk, lanes] = dk[pl.ds(start, chunk), :]
                out[chunk:2 * chunk, lanes] = dv[pl.ds(start, chunk), :]
            return 0

        lax.fori_loop(0, heads, one_head, 0)

    operands = [*near, *kv, *qd, *halos, words, masks, gain]
    return call(
        kernel, [place, window_ext, text_len], [(x, "vmem") for x in operands],
        [((1, slot, width), BF16, "vmem")] * 4
        + [((2, 2 * tile, width), F32, "vmem"), ((2, 128), F32, "vmem")]
        + [((8, width), F32, "vmem")] * 2
        + [((2 * chunk, width), F32, "vmem")] * chunks,
        [
            pltpu.VMEM((video + text_count, 256), BF16),
            pltpu.VMEM((video + text_count, 128), BF16),
            pltpu.VMEM((video, 128), F32),
            pltpu.VMEM((2 * tile, 256), BF16),
            pltpu.VMEM((2 * tile, 128), BF16),
            pltpu.VMEM((2 * tile, 128), F32),
            pltpu.VMEM((2 * tile, 128), F32),
            pltpu.VMEM((2 * tile + text_count, 128), F32),
            pltpu.VMEM((2 * tile + text_count, 128), F32),
            pltpu.VMEM((2 * tile, 128), BF16),
        ],
    )


def edges(place, window_ext, own, messages, near, kv, halos, masks, gain):
    _, slot, width = near[0].shape
    heads = width // 128
    tile = 2 * slot
    scale = 128 ** -0.5

    def kernel(place_ref, ext_ref, *refs):
        own_ref, before_ref, after_ref, n0, n1, kv2, kv3, ha, hb = refs[:9]
        mask_ref, gain_ref, o0, o1, o2, o3 = refs[9:15]
        kn, vs, kx, kr, qn, grads, ends = refs[15:]
        g, p, last = place_ref[0], place_ref[1], place_ref[2]
        gq, gk = gain_ref[0:1, :], gain_ref[1:2, :]
        at = lambda start: pl.ds(pl.multiple_of(start, slot), slot)
        own_at, halo_at = spots(g, slot, 0, tile)
        for t in range(2):
            qn[t * tile:(t + 1) * tile, 128:] = mask_ref[2].astype(BF16)

        def one_head(h, _):
            lanes = pl.ds(pl.multiple_of(h * 128, 128), 128)
            head = heads * g + h
            e0, e1, e2 = ext_ref[0, head], ext_ref[1, head].astype(F32), ext_ref[2, head].astype(F32)
            for r, start in zip((n0, n1, kv2, kv3), own_at):
                hat, inverse = unit(r[0, :, lanes])
                kx[at(start), :] = hat
                kr[at(start), :] = jnp.broadcast_to(inverse, hat.shape)
                kn[at(start), :128] = (hat * gk).astype(BF16)
                vs[at(start), :] = r[1, :, lanes]
            for r, start in zip((ha.at[0], ha.at[1], hb.at[0], hb.at[1]), halo_at):
                qn[at(start), :128] = (unit(r[0, :, lanes])[0] * gq).astype(BF16)
                grads[at(start), :] = r[1, :, lanes]
            close = (mask_ref[0] <= e1) & (mask_ref[1] <= e2) & (e0 >= 1)
            for t in range(2):
                kn[t * tile:(t + 1) * tile, 128:] = hidden(close & ((p > 0) if t == 0 else (p < last)))
            for t, message in enumerate((before_ref, after_ref)):
                rows = slice(t * tile, (t + 1) * tile)
                top, share, delta = [
                    jnp.concatenate([message[i:i + 1, lanes] for i in (n, n + 1)], axis=1)
                    for n in (0, 2, 4)
                ]
                query, grad = qn[rows, :], grads[rows, :]
                probs = jnp.exp2((dot(kn[rows, :], query, (1, 1)) - top) * (scale * LOG2E)) * share
                prob_grad = dot(vs[rows, :], grad, (1, 1))
                score_grad = (probs * (prob_grad - delta)).astype(BF16)
                value_sum = own_ref[1, rows, lanes] + dot(probs.astype(BF16), grad, (1, 0))
                key_sum = own_ref[0, rows, lanes] + dot(score_grad, query[:, :128], (1, 0)) * scale
                hat = kx[rows, :]
                weighted = key_sum * gk
                inner = jnp.mean(weighted * hat, axis=-1, keepdims=True)
                ends[0, rows, :] = (kr[rows, :] * (weighted - hat * inner)).astype(BF16)
                ends[1, rows, :] = value_sum.astype(BF16)
            for j, out in enumerate((o0, o1, o2, o3)):
                out[0, :, lanes] = ends[0, at(own_at[j]), :]
                out[1, :, lanes] = ends[1, at(own_at[j]), :]
            return 0

        lax.fori_loop(0, heads, one_head, 0)

    operands = [own, *messages, *near, *kv, *halos, masks, gain]
    return call(
        kernel, [place, window_ext], [(x, "vmem") for x in operands],
        [((2, slot, width), BF16, "vmem")] * 4,
        [
            pltpu.VMEM((2 * tile, 256), BF16),
            pltpu.VMEM((2 * tile, 128), BF16),
            pltpu.VMEM((2 * tile, 128), F32),
            pltpu.VMEM((2 * tile, 128), F32),
            pltpu.VMEM((2 * tile, 256), BF16),
            pltpu.VMEM((2 * tile, 128), BF16),
            pltpu.VMEM((2, 2 * tile, 128), BF16),
        ],
    )


def text_chunk(parts, gains):
    rows, width = parts[0].shape

    def kernel(*refs):
        sums, tails, out_ref = refs[:len(parts)], refs[len(parts):-1], refs[-1]
        total = sums[0][...]
        for ref in sums[1:]:
            total = total + ref[...]
        out_ref[:rows, :] = total.astype(BF16)
        out_ref[rows:, :] = jnp.zeros((8, width), BF16)
        rest = tails[0][...]
        for ref in tails[1:]:
            rest = rest + ref[...]
        for i in range(3):
            part = rest.astype(BF16)
            out_ref[rows + 2 * i:rows + 2 * i + 2, :128] = part
            rest = rest - part.astype(F32)

    return call(kernel, [], [(x, "vmem") for x in parts + gains], [((rows + 8, width), BF16, "vmem")])[0]


def text_columns(place, members, firsts, rests, earlier=None):
    chunks, padded, width = rests[0].shape
    chunks, rows = chunks + 1, (padded - 8) // 2
    shape = (rows * chunks, 4 * width)

    def kernel(place_ref, *refs):
        key_ref, value_ref, gain_ref, hold, sems = refs[len(refs) - 5:]
        gains = refs[4][...] if earlier is not None else jnp.zeros((2, 128), F32)
        copies = []
        for n, j in enumerate(members):
            for d in range(chunks):
                piece = refs[n] if d == 0 else refs[2 + n].at[d - 1]
                start = pl.multiple_of(lax.rem(place_ref[1] + (chunks - d), chunks) * rows, 8)
                for i in range(2):
                    hold[n, i, pl.ds(start, rows), :] = piece[i * rows:(i + 1) * rows].astype(F32)
                tail = piece[2 * rows:, :128].astype(F32)
                gains = gains + (tail[0:2] + tail[2:4] + tail[4:6])
            start = pl.multiple_of((place_ref[0] ^ j) * width, 128)
            for i, out in enumerate((key_ref, value_ref)):
                copies.append(pltpu.make_async_copy(hold.at[n, i], out.at[:, pl.ds(start, width)], sems.at[n, i]))
                copies[-1].start()
        gain_ref[...] = gains
        for copy in copies:
            copy.wait()

    more = [] if earlier is None else [(earlier[2], "vmem"), (earlier[0], "hbm"), (earlier[1], "hbm")]
    return call(
        kernel, [place], [(x, "vmem") for x in (*firsts, *rests)] + more,
        [(shape, F32, "hbm"), (shape, F32, "hbm"), ((2, 128), F32, "vmem" if earlier is None else "out")],
        [pltpu.VMEM((2, 2, rows * chunks, width), F32), pltpu.SemaphoreType.DMA((2, 2))],
        {} if earlier is None else {6: 0, 7: 1},
    )


def local(queries, keys, values, text_keys, text_values, gain_q, gain_k, window_ext, text_len, out_grad):
    head_count = window_ext.shape[0]
    frames, half, columns, features = queries.shape[1:]
    text_count = text_keys.shape[1]
    peers, heights, samples = lax.axis_size("tm"), lax.axis_size("height"), lax.axis_size("dp")
    quads = peers // 2
    assert frames == TILE_F and heights == 2 and peers % 2 == 0 and quads >= 3
    assert features == 128 * head_count and head_count % 4 == 0
    assert half % TILE_H == 0 and columns % TILE_W == 0 and text_count % (8 * quads) == 0
    axes = ("tm", "height")
    me = lax.axis_index("tm")
    quad = me // 2
    member = (me % 2) * 2 + lax.axis_index("height")
    place = jnp.stack([member, quad, jnp.full_like(quad, quads - 1)]).astype(jnp.int32)

    def permute(x, pairs, over=axes):
        return lax.ppermute(x, over, pairs)

    def swap(x, j):
        return permute(x, [(4 * n + m, 4 * n + (m ^ j)) for n in range(quads) for m in range(4)])

    def move(x, step):
        pairs = [(4 * n + m, 4 * (n + step(m // 2)) + m) for n in range(quads) for m in range(4)]
        return permute(x, [(i, j) for i, j in pairs if 0 <= j < 4 * quads])

    def turn(x, d):
        return permute(x, [(4 * n + m, 4 * ((n + d) % quads) + m) for n in range(quads) for m in range(4)])

    out_a, out_b = (lambda a: 2 * a - 1), (lambda a: 1 - 2 * a)
    flat = [x.reshape(-1, features) for x in (keys, values, queries, out_grad)]
    table, space = spatial(half, columns, columns * half * frames)

    near0, near1, kv2, kv3, qd2, qd3 = pack(
        place, flat, [(0, (0, 1, 2, 3)), (1, (0, 1, 2, 3)), (2, (0, 1)), (3, (0, 1)), (2, (2, 3)), (3, (2, 3))]
    )
    kv_in = [swap(kv2, 2), swap(kv3, 3)]
    qd_in = [swap(qd2, 2), swap(qd3, 3)]
    words, gain, masks = stage(
        place, (text_keys[0], text_values[0]), (gain_q.reshape(1, -1), gain_k.reshape(1, -1)), table
    )
    near = [near0, swap(near1, 1)]
    kv_a, qd_a = join([[(x, 0, 2) for x in near], [(x, 2, 4) for x in near]])
    (kv_b,) = join([[(x, 0, 2) for x in kv_in]])
    (qd_b,) = join([[(x, 0, 2) for x in qd_in]])
    kv_halos = [move(kv_a, out_a), move(kv_b, out_b)]
    qd_halos = [move(qd_a, out_a), move(qd_b, out_b)]
    ext = window_ext.T

    oq0, oq1, oq2, oq3, own, gains, stats0, stats1, *texts = attention(
        place, ext, text_len, near, kv_in, qd_in, kv_halos, words, masks, space, gain, quads
    )
    after, before = move(stats0, lambda a: -1), move(stats1, lambda a: 1)
    text_in = [turn(texts[i], i) for i in range(1, quads)]
    others = [permute(gains, [(n, (n + i) % samples) for n in range(samples)], "dp") for i in range(1, samples)]
    oq_in = [swap(x, j) for x, j in zip((oq1, oq2, oq3), (1, 2, 3))]
    (query_out,) = unpack(place, [oq0] + oq_in)
    chunk = text_chunk([texts[0]] + text_in, [gains] + others)
    rest = jnp.stack([turn(chunk, i) for i in range(1, quads)])
    across = swap(chunk, 2)
    side1 = swap(chunk, 1)
    side3 = swap(across, 1)
    ends = edges(place, ext, own, (before, after), near, kv_in, qd_halos, masks, gain)
    ends_in = [swap(ends[j], j) for j in (1, 2, 3)]
    across_rest = swap(rest, 2)
    side1_rest = swap(rest, 1)
    side3_rest = swap(across_rest, 1)
    key_out, value_out = unpack(place, [ends[0]] + ends_in)
    early = text_columns(place, (0, 1), (chunk, side1), (rest, side1_rest))
    text_key_out, text_value_out, gain_out = text_columns(
        place, (2, 3), (across, side3), (across_rest, side3_rest), early
    )
    shape = queries.shape
    return (
        query_out.reshape(shape),
        key_out.reshape(shape),
        value_out.reshape(shape),
        text_key_out[None],
        text_value_out[None],
        gain_out,
    )


def solution(mesh):
    tokens = P("dp", "tm", "height", None, None)
    words = P("dp", None, None)

    return jax.shard_map(
        local,
        mesh=mesh,
        in_specs=(tokens, tokens, tokens, words, words, P(), P(), P(), P("dp"), tokens),
        out_specs=(tokens, tokens, tokens, words, words, P()),
        check_vma=False,
    )
```
